32 devices in a mesh: aux: 4 (over z), pair: 8 (over y, x, core).
Axes of the slice: x: 2, y: 2, z: 4, core: 2. Of those that a mesh axis runs over, the one named last changes fastest.
Arguments:
- b_three: bfloat16 [4096, 2048], P('pair', 'aux'), may hold values from -0.13183594 to 0.13183594
- metric: bfloat16 [2048, 2048], P(None, 'aux'), may hold values from -1 to 2
- aux_map: int32 [64, 32], P('pair', 'aux'), may hold values 0 or 1
- domains: int32 [80, 4], replicated, may hold values from 0 to 63, as said below
- counts: int32 [80], P('pair'), may hold values from 1 to 4, as said below
Outputs:
- pair_integrals: float32 [80, 256, 256], P('pair', 'aux')
The draws below stay inside these ranges and needn't reach their ends.
Inputs may be any that keep to these rules, and one draw needn't show every extreme that they name: `domains`: of the 40 slots of the pairs of one index of pair (pairs q * 10 to (q + 1) * 10 - 1), at most 5 name blocks held by one index of pair (blocks o * 8 to (o + 1) * 8 - 1), and exactly 5 for some such index in every draw. `counts`: slots at or past a pair's count are padding.
All inputs are finite; a program needn't handle non-finite values. No bound on the sum of `aux_map` on one device may be relied on, other than what follows from the above.
Results may differ from the reference program's by a relative error of at most 0.00079.
Values may be sent and summed in bfloat16 or wider, within the bound.
A program may use at most 64 MiB of HBM per device.

```python
import jax
import jax.numpy as jnp
from jax import lax

AUXW = 64
CW = 64
DMAX = 4
DB_DEV = 8
PAIR_DEV = 10
NAB = 32
NA = 2048
NDB = 64
NPAIRS = 80
SLOTS = 40
CAP = 5
N_PAIR = 8


def draw_metric(key, part):
    noise = jax.random.normal(key, (NA, NA), jnp.float32)
    return (jnp.eye(NA, dtype=jnp.float32) + 0.5 * noise * NA ** (-0.5)).astype(jnp.bfloat16)


def draw_domains(key, part):
    device_keys = jax.random.split(jax.random.fold_in(key, 11), N_PAIR)

    def one_device(sub_key):
        shuffled = jax.random.permutation(sub_key, CAP * N_PAIR)
        return (shuffled[:SLOTS] % N_PAIR).astype(jnp.int32)
    owners = jax.vmap(one_device)(device_keys)
    local_block = jax.random.randint(jax.random.fold_in(key, 12), (N_PAIR, SLOTS), 0, DB_DEV)
    return (owners * DB_DEV + local_block).reshape(NPAIRS, DMAX).astype(jnp.int32)


def draw_counts(key, part):
    device_level = jax.random.randint(jax.random.fold_in(key, 21), (N_PAIR, 1), 1, DMAX + 1)
    raw_counts = jax.random.randint(jax.random.fold_in(key, 22), (N_PAIR, PAIR_DEV), 1, DMAX + 1)
    counts = jnp.minimum(raw_counts, device_level).reshape(NPAIRS)
    full_pair = jax.random.randint(jax.random.fold_in(key, 23), (), 0, NPAIRS)
    return counts.at[full_pair].set(DMAX).astype(jnp.int32)


def place_ends(result, rng, smallest, largest):
    longest = result.shape.index(max(result.shape))
    spots = []
    for shift in (0, 1):
        where = [jax.random.randint(jax.random.fold_in(rng, axis), (), 0, length) for axis, length in enumerate(result.shape)]
        where[longest] = (where[longest] + shift) % result.shape[longest]
        spots.append(tuple(where))
    return result.at[spots[0]].set(smallest).at[spots[1]].set(largest)


def shard_levels(own_key, shape, pieces, low, largest):
    gain = 1.0
    for dim, shards_of in pieces:
        draws = jax.random.uniform(jax.random.fold_in(jax.random.fold_in(own_key, 6), dim), (shards_of,), jnp.float32, low / len(pieces), largest / len(pieces))
        gain = gain * jnp.repeat(jnp.exp(draws), shape[dim] // shards_of).reshape((-1,) + (1,) * (len(shape) - 1 - dim))
    return gain


def gaussian(key, shape, width, most, cuts=(), kind=jnp.bfloat16):
    entries = jax.random.normal(key, shape, jnp.float32) * width
    if len(cuts) > 0:
        entries = shard_levels(key, shape, cuts, -0.22, 0.18) * entries
    return jnp.clip(entries, min=-most, max=most).astype(kind)


def setup_inputs(seed: int = 0) -> dict:
    keys = jax.random.split(jax.random.key(seed), 6)
    return {
        "b_three": gaussian(keys[0], (NDB * CW, NA), (NA ** -0.5), 0.13183594, ((0, 8), (1, 4))),
        "metric": draw_metric(jax.random.fold_in(keys[5], 71), 0),
        "aux_map": place_ends((jax.random.randint(keys[2], (NDB, NAB), 0, 4) < 3).astype(jnp.int32), jax.random.fold_in(keys[2], 1), 0, 1),
        "domains": draw_domains(jax.random.fold_in(keys[5], 71), 0),
        "counts": draw_counts(jax.random.fold_in(keys[5], 71), 0),
    }


def reference(b_three, metric, aux_map, domains, counts):
    keep_mask = aux_map.astype(jnp.bfloat16)
    row_total, aux_total = b_three.shape
    masked = (b_three.reshape(NDB, CW, NAB, AUXW) * keep_mask[:, None, :, None]).reshape(row_total, aux_total)
    fitted = jnp.dot(masked, metric, preferred_element_type=jnp.float32).astype(jnp.bfloat16)
    block_table = fitted.reshape(NDB, CW, aux_total)
    slot_of = jnp.arange(DMAX * CW, dtype=jnp.int32) // CW

    def one_pair(entry):
        block_names, live_count = entry
        stacked = block_table[block_names].reshape(DMAX * CW, aux_total).astype(jnp.float32)
        product = jnp.dot(stacked, stacked.T, preferred_element_type=jnp.float32)
        live_rows = slot_of < live_count
        return jnp.where(live_rows[:, None] & live_rows[None, :], product, jnp.zeros_like(product))

    return lax.map(one_pair, (domains, counts))
```

```python
import functools

import jax
import jax.numpy as jnp
from jax import lax
from jax.experimental import pallas as pl
from jax.experimental.pallas import tpu as pltpu
from jax.sharding import PartitionSpec as P

MESH = pl.DeviceIdType.MESH


def line_kernel(n, n_pair, split, b_hbm, metric_hbm, map_ref, dom_ref, out_ref, diag_ref,
           b_raw, b_ref, metric_ref, in_sem, b_all, table, g_send, g_recv, d_own, d_recv,
           r_s, r_r, l_s, l_r, p_s, p_r, f_s, f_r, g_s, g_r, d_s, d_r):
    chunks, rows, depth = b_hbm.shape
    pairs, slab, width = out_ref.shape
    slots = dom_ref.shape[0]
    chips = n_pair // 2
    z = lax.axis_index("aux")
    q = lax.axis_index("pair")
    core = lax.rem(q, 2)
    chip = q // 2
    partner = q + 1 - 2 * core
    has_right = z + 1 < n
    has_left = z > 0

    def chip_at(k):
        return lax.rem(chip + k + chips, chips) * 2 + core

    load_b = pltpu.make_async_copy(b_hbm.at[0], b_raw.at[0], in_sem.at[0])
    load_rest = pltpu.make_async_copy(b_hbm.at[1:], b_raw.at[1:], in_sem.at[2])
    load_metric = pltpu.make_async_copy(metric_hbm, metric_ref, in_sem.at[1])
    load_b.start()
    load_rest.start()
    load_metric.start()
    barrier = pltpu.get_barrier_semaphore()
    for near_z, there in ((z + 1, has_right), (z - 1, has_left)):
        @pl.when(there)
        def _():
            pl.semaphore_signal(barrier, inc=1, device_id=(near_z, q), device_id_type=MESH)
    for k in range(1, chips):
        pl.semaphore_signal(barrier, inc=1, device_id=(z, chip_at(k)), device_id_type=MESH)
    pl.semaphore_signal(barrier, inc=1, device_id=(z, partner), device_id_type=MESH)
    aux_blocks = map_ref.shape[1]
    spread_row = lax.broadcasted_iota(jnp.int32, (aux_blocks, depth), 0)
    spread_col = lax.broadcasted_iota(jnp.int32, (aux_blocks, depth), 1) // (depth // aux_blocks)
    keep = jnp.dot(map_ref[...].astype(jnp.float32), (spread_row == spread_col).astype(jnp.float32),
                   preferred_element_type=jnp.float32)
    def mask(c):
        b_ref[c] = (b_raw[c].astype(jnp.float32) * keep[c // split:c // split + 1, :]).astype(b_ref.dtype)
    load_b.wait()
    mask(0)
    pl.semaphore_wait(barrier, chips + has_right.astype(jnp.int32) + has_left.astype(jnp.int32))

    def remote(src, dst, send, recv, device):
        return pltpu.make_async_remote_copy(
            src_ref=src, dst_ref=dst, send_sem=send, recv_sem=recv, device_id=device, device_id_type=MESH)

    def along(h, c, right):
        step = 1 if right else -1
        origin = z - step * h
        send, recv = (r_s, r_r) if right else (l_s, l_r)
        src = b_ref.at[c] if h == 0 else b_all.at[origin, c]
        return remote(src, b_all.at[origin, c], send.at[h, c], recv.at[h, c], (z + step, q))

    def arrival(h, c, right):
        recv = r_r if right else l_r
        origin = z - 1 - h if right else z + 1 + h
        return remote(b_ref.at[c], b_all.at[origin, c], recv.at[h, c], recv.at[h, c], (z, partner))

    def own_chunk(c):
        for right in (True, False):
            @pl.when(has_right if right else has_left)
            def _():
                along(0, c, right).start()

    def relay(h, c):
        for right in (True, False):
            came = z - h >= 0 if right else z + h < n

            @pl.when(came)
            def _():
                arrival(h - 1, c, right).wait_recv()

                if h < n - 1:
                    @pl.when(has_right if right else has_left)
                    def _():
                        along(h, c, right).start()

    def spread(k, c):
        target = partner if k == 0 else chip_at(k)
        return remote(table.at[q, c], table.at[q, c], p_s.at[k, c], p_r.at[k, c], (z, target))

    def forward(k, c):
        origin = chip_at(-k)
        return remote(table.at[origin, c], table.at[origin, c], f_s.at[k, c], f_r.at[k, c], (z, partner))

    def fit(c):
        total = jnp.dot(b_ref[c], metric_ref[pl.ds(pl.multiple_of(z * depth, depth), depth), :],
                        preferred_element_type=jnp.float32)
        for k in range(1, n):
            origin = lax.rem(z + k, n)
            total += jnp.dot(b_all[origin, c],
                             metric_ref[pl.ds(pl.multiple_of(origin * depth, depth), depth), :],
                             preferred_element_type=jnp.float32)
        table[q, c] = total.astype(table.dtype)
        for k in list(range(1, chips)) + [0]:
            spread(k, c).start()

    def pass_on(c):
        for k in range(1, chips):
            spread_in = remote(table.at[chip_at(-k), c], table.at[chip_at(-k), c],
                               p_s.at[k, c], p_r.at[k, c], (z, partner))
            spread_in.wait_recv()
            forward(k, c).start()

    own_chunk(0)
    load_rest.wait()
    for c in range(1, chunks):
        mask(c)
    load_metric.wait()

    def stage(step, carry):
        @pl.when(step + 1 < chunks)
        def _():
            own_chunk(step + 1)
        for h in range(n - 1, 0, -1):
            @pl.when((step + 1 >= h) & (step + 1 - h < chunks))
            def _():
                relay(h, step + 1 - h)

        @pl.when((step + 2 >= n) & (step + 2 - n < chunks))
        def _():
            fit(step + 2 - n)

        @pl.when((step >= n) & (step - n < chunks))
        def _():
            pass_on(step - n)
        return carry

    lax.fori_loop(0, chunks + n, stage, 0)

    def finish(c, carry):
        remote(table.at[partner, c], table.at[partner, c], p_s.at[0, c], p_r.at[0, c],
               (z, partner)).wait_recv()
        for k in range(1, chips):
            origin = chip_at(-k) + 1 - 2 * core
            remote(table.at[origin, c], table.at[origin, c], f_s.at[k, c], f_r.at[k, c],
                   (z, partner)).wait_recv()
        return carry

    lax.fori_loop(0, chunks, finish, 0)

    row_of = lax.broadcasted_iota(jnp.int32, (width, width), 0)
    col_of = lax.broadcasted_iota(jnp.int32, (width, width), 1)

    def gram_copy(k, p):
        return remote(g_send.at[lax.rem(z + k, n), p], g_recv.at[k - 1, p],
                      g_s.at[k - 1, p], g_r.at[k - 1, p], (lax.rem(z + k, n), q))

    def gram(p, carry):
        blocks = []
        for s in range(slots):
            name = dom_ref[s, q * pairs + p]
            local = lax.rem(name, chunks // split) * split
            for t in range(split):
                blocks.append(table[name // (chunks // split), local + t])
        stack = jnp.concatenate(blocks, axis=0)
        full = lax.dot_general(stack, stack, (((1,), (1,)), ((), ())), preferred_element_type=jnp.float32)
        d_own[p] = jnp.sum(jnp.where(row_of == col_of, full, 0.0), axis=0, keepdims=True)
        for d in range(n):
            part = full[d * slab:(d + 1) * slab]

            @pl.when(z == d)
            def _():
                out_ref[p] = part

            @pl.when(z != d)
            def _():
                g_send[d, p] = part.astype(g_send.dtype)
        for k in range(1, n):
            gram_copy(k, p).start()
        return carry

    lax.fori_loop(0, pairs, gram, 0)

    def diag_copy(k):
        return remote(d_own, d_recv.at[k - 1], d_s.at[k - 1], d_r.at[k - 1], (lax.rem(z + k, n), q))

    for k in range(1, n):
        diag_copy(k).start()
    def add(p, carry):
        total = out_ref[p]
        for k in range(1, n):
            gram_copy(k, p).wait_recv()
            total += g_recv[k - 1, p].astype(jnp.float32)
        out_ref[p] = total
        return carry

    lax.fori_loop(0, pairs, add, 0)
    for k in range(1, n):
        diag_copy(k).wait_recv()

    diag = d_own[...]
    for k in range(1, n):
        diag += d_recv[k - 1]
    diag_ref[...] = diag

    def drain(c, carry):
        for right in (True, False):
            for h in range(n - 1):
                goes = (has_right & (z - h >= 0)) if right else (has_left & (z + h < n))

                @pl.when(goes)
                def _():
                    along(h, c, right).wait_send()
        for k in range(chips):
            spread(k, c).wait_send()
        for k in range(1, chips):
            forward(k, c).wait_send()
        return carry

    lax.fori_loop(0, chunks, drain, 0)

    def drain_gram(p, carry):
        for k in range(1, n):
            gram_copy(k, p).wait_send()
        return carry

    lax.fori_loop(0, pairs, drain_gram, 0)
    for k in range(1, n):
        diag_copy(k).wait_send()


def box_kernel(n, n_pair, split, b_hbm, metric_hbm, map_ref, dom_ref, out_ref, diag_ref,
               b_raw, b_ref, metric_ref, in_sem, b_all, table, far_metric, fit_part,
               m_s, m_r, o_s, o_r, w_s, w_r, y_s, y_r,
               tp_s, tp_r, tt_s, tt_r, tf_s, tf_r, mp_s, mp_r, mt_s, mt_r, mf_s, mf_r,
               g_send, g_recv, d_own, d_recv, g_s, g_r, d_s, d_r,
               g_far, far_out, far_recv, far_send, late_send, late_recv, x_s, x_r, c_s):
    chunks, rows, depth = b_hbm.shape
    pairs, slab, width = out_ref.shape
    slots = dom_ref.shape[0]
    parts = far_metric.shape[1]
    z = lax.axis_index("aux")
    q = lax.axis_index("pair")
    core = lax.rem(q, 2)
    chip = q // 2
    flip = 1 - 2 * core
    partner = q + flip
    near_x = (chip + 1 - 2 * lax.rem(chip, 2)) * 2 + core
    near_y = lax.rem(chip + 2, 4) * 2 + core
    corner = (lax.rem(chip + 2, 4) + 1 - 2 * lax.rem(chip, 2)) * 2 + core
    mate = z + 1 - 2 * lax.rem(z, 2)
    other = n - 1 - z
    low = z < 2
    is_end = (z == 0) | (z == n - 1)
    is_mid = jnp.logical_not(is_end)

    load_b = pltpu.make_async_copy(b_hbm.at[0], b_raw.at[0], in_sem.at[0])
    load_rest = pltpu.make_async_copy(b_hbm.at[1:], b_raw.at[1:], in_sem.at[2])
    load_metric = pltpu.make_async_copy(metric_hbm, metric_ref, in_sem.at[1])
    load_b.start()
    load_rest.start()
    load_metric.start()
    barrier = pltpu.get_barrier_semaphore()
    for there in ((mate, q), (z, partner), (z, near_x), (z, near_y)):
        pl.semaphore_signal(barrier, inc=1, device_id=there, device_id_type=MESH)

    @pl.when(is_mid)
    def _():
        pl.semaphore_signal(barrier, inc=1, device_id=(other, q), device_id_type=MESH)

    aux_blocks = map_ref.shape[1]
    spread_row = lax.broadcasted_iota(jnp.int32, (aux_blocks, depth), 0)
    spread_col = lax.broadcasted_iota(jnp.int32, (aux_blocks, depth), 1) // (depth // aux_blocks)
    keep = jnp.dot(map_ref[...].astype(jnp.float32), (spread_row == spread_col).astype(jnp.float32),
                   preferred_element_type=jnp.float32)

    def mask(c):
        b_ref[c] = (b_raw[c].astype(jnp.float32) * keep[c // split:c // split + 1, :]).astype(b_ref.dtype)

    load_b.wait()
    mask(0)
    pl.semaphore_wait(barrier, 4 + is_mid.astype(jnp.int32))

    def remote(src, dst, send, recv, device):
        return pltpu.make_async_remote_copy(
            src_ref=src, dst_ref=dst, send_sem=send, recv_sem=recv, device_id=device, device_id_type=MESH)

    def swap(c, origin=None):
        src = b_ref.at[c]
        return remote(src, b_all.at[z if origin is None else origin, c], m_s.at[c], m_r.at[c], (mate, q))

    def own(c, origin=None):
        return remote(b_ref.at[c], b_all.at[z if origin is None else origin, c], o_s.at[0, c], o_r.at[0, c], (other, q))

    def relay(c, origin=None):
        at = b_all.at[mate if origin is None else origin, c]
        return remote(at, at, o_s.at[1, c], o_r.at[1, c], (other, q))

    def half_fit(c):
        return remote(fit_part.at[c], fit_part.at[c], w_s.at[c], w_r.at[c], (mate, q))

    far_first = jnp.where(z == 0, n // 2, 0) * depth
    piece = parts * rows

    def metric_part(t):
        start = pl.multiple_of(far_first + q * piece + t * rows, rows)
        return remote(metric_ref.at[pl.ds(start, rows)], far_metric.at[q, t], y_s.at[t], y_r.at[t], (mate, q))

    def in_plane(buf, p_s, p_r, t_s, t_r, f_s, f_r):
        half = rows // 2

        def give(k, c):
            target = (partner, near_x, near_y)[k]
            return remote(buf.at[q, c], buf.at[q, c], p_s.at[k, c], p_r.at[k, c], (z, target))

        def turn(k, c):
            at = buf.at[(near_x, near_y)[k], c, pl.ds(k * half, half)]
            return remote(at, at, t_s.at[k, c], t_r.at[k, c], (z, (near_y, near_x)[k]))

        def forward(k, c):
            at = buf.at[(near_x, near_y, corner)[k], c]
            return remote(at, at, f_s.at[k, c], f_r.at[k, c], (z, partner))

        def share(c):
            for k in (1, 2, 0):
                give(k, c).start()

        def pass_on(c):
            for k in (0, 1):
                at = buf.at[(near_x, near_y)[k], c]
                remote(at, at, p_s.at[k + 1, c], p_r.at[k + 1, c], (z, partner)).wait_recv()
                turn(k, c).start()
                forward(k, c).start()

        def pass_corner(c):
            for k in (0, 1):
                at = buf.at[corner, c, pl.ds(k * half, half)]
                remote(at, at, t_s.at[k, c], t_r.at[k, c], (z, partner)).wait_recv()
            forward(2, c).start()

        def finish(c):
            at = buf.at[partner, c]
            remote(at, at, p_s.at[0, c], p_r.at[0, c], (z, partner)).wait_recv()
            for k in range(3):
                at = buf.at[(near_x, near_y, corner)[k] + flip, c]
                remote(at, at, f_s.at[k, c], f_r.at[k, c], (z, partner)).wait_recv()

        def drain(c):
            for k in range(3):
                give(k, c).wait_send()
                forward(k, c).wait_send()
            for k in range(2):
                turn(k, c).wait_send()

        return share, pass_on, pass_corner, finish, drain

    share, pass_on, pass_corner, finish, drain = in_plane(table, tp_s, tp_r, tt_s, tt_r, tf_s, tf_r)
    m_share, m_pass_on, m_pass_corner, m_finish, m_drain = in_plane(far_metric, mp_s, mp_r, mt_s, mt_r, mf_s, mf_r)

    def metric_rows(origin):
        return metric_ref[pl.ds(pl.multiple_of(origin * depth, depth), depth), :]

    def arrive(c):
        own(c, other).wait_recv()
        relay(c, n - 1 - mate).wait_recv()

    def fit_mid(c):
        total = jnp.dot(b_ref[c], metric_rows(z), preferred_element_type=jnp.float32)
        for origin in (mate, other, n - 1 - mate):
            total += jnp.dot(b_all[origin, c], metric_rows(origin), preferred_element_type=jnp.float32)
        table[q, c] = total.astype(table.dtype)
        share(c)

    def fit_far(c):
        far = jnp.where(low, n // 2, 0)
        group = 2 * piece
        per_slice = depth // group
        total = None
        for j in range(n // 2 * per_slice):
            lhs = b_all[far + j // per_slice, c, :, (j % per_slice) * group:(j % per_slice + 1) * group]
            rhs = jnp.concatenate([far_metric[2 * j + k, t] for k in range(2) for t in range(parts)], axis=0)
            term = jnp.dot(lhs, rhs, preferred_element_type=jnp.float32)
            total = term if total is None else total + term
        fit_part[c] = total.astype(fit_part.dtype)
        half_fit(c).start()

    def fit_end(c):
        swap(c, mate).wait_recv()
        total = jnp.dot(b_ref[c], metric_rows(z), preferred_element_type=jnp.float32)
        total += jnp.dot(b_all[mate, c], metric_rows(mate), preferred_element_type=jnp.float32)
        half_fit(c).wait_recv()
        table[q, c] = (total + fit_part[c].astype(jnp.float32)).astype(table.dtype)
        share(c)

    @pl.when(is_mid)
    def _():
        own(0).start()

    swap(0).start()
    load_rest.wait()
    for c in range(1, chunks):
        mask(c)

        @pl.when(is_mid)
        def _():
            if c < 2:
                own(c).start()
            swap(c).start()

    load_metric.wait()

    @pl.when(is_end)
    def _():
        for c in range(1, chunks):
            if c <= parts:
                metric_part(c - 1).start()
            swap(c).start()

        def stage(c, carry):
            @pl.when(c < chunks)
            def _():
                fit_end(c)

            @pl.when((c >= 1) & (c < chunks + 1))
            def _():
                pass_on(c - 1)

            @pl.when(c >= 2)
            def _():
                pass_corner(c - 2)
            return carry

        lax.fori_loop(0, chunks + 2, stage, 0)

    @pl.when(is_mid)
    def _():
        ready = parts + 2

        def stage(s, carry):
            @pl.when(s < chunks)
            def _():
                swap(s, mate).wait_recv()
                relay(s).start()

            @pl.when(s + 2 < chunks)
            def _():
                own(s + 2).start()

            @pl.when((s >= 1) & (s <= parts))
            def _():
                t = s - 1
                at = far_metric.at[q, t]
                remote(at, at, y_s.at[t], y_r.at[t], (z, partner)).wait_recv()
                m_share(t)

            @pl.when((s >= 2) & (s < parts + 2))
            def _():
                m_pass_on(s - 2)

            @pl.when((s >= 3) & (s < parts + 3))
            def _():
                m_pass_corner(s - 3)

            @pl.when((s >= 1) & (s <= chunks))
            def _():
                arrive(s - 1)

            first = 2 * (s - ready)
            late_step = first >= s

            @pl.when((s > ready) & late_step & (s <= chunks))
            def _():
                fit_far(s - 1)

            @pl.when((s >= 1) & (s <= chunks))
            def _():
                fit_mid(s - 1)

            @pl.when((s >= 2) & (s < chunks + 2))
            def _():
                pass_on(s - 2)

            @pl.when(s >= 3)
            def _():
                pass_corner(s - 3)

            @pl.when(s == ready)
            def _():
                for t in range(parts):
                    m_finish(t)

            @pl.when((s >= ready) & jnp.logical_not(late_step))
            def _():
                for c in (first, first + 1):
                    @pl.when((c < s) & (c < chunks))
                    def _():
                        fit_far(c)
            return carry

        lax.fori_loop(0, chunks + 3, stage, 0)

    def finish_all(c, carry):
        finish(c)
        return carry

    lax.fori_loop(0, chunks, finish_all, 0)

    row_of = lax.broadcasted_iota(jnp.int32, (width, width), 0)
    col_of = lax.broadcasted_iota(jnp.int32, (width, width), 1)

    half = width // 2

    def near(p):
        return remote(g_send.at[0, p], g_recv.at[0, p], g_s.at[0, p], g_r.at[0, p], (mate, q))

    def late(p):
        return remote(late_send.at[p], late_recv.at[p], g_s.at[0, p], g_r.at[0, p], (mate, q))

    def to_mid(p):
        return remote(far_out.at[p], far_recv.at[p], x_s.at[p], x_r.at[p], (mate, q))

    def across(j, p):
        return remote(far_send.at[j, p], g_recv.at[1, p], c_s.at[j, p], g_r.at[1, p],
                      (jnp.where(z < 2, 2, 0) + j, q))

    def combine(below):
        def one(p, carry):
            to_mid(p).wait_recv()
            top = far_recv[p, 0:half].astype(jnp.float32)
            bottom = far_recv[p, half:width].astype(jnp.float32)
            parts = (top.T, bottom) if below else (top, bottom.T)
            value = (g_far[p] + jnp.concatenate(parts, axis=1)).astype(far_send.dtype)
            for j in ((1, 0) if below else (0, 1)):
                far_send[j, p] = value[j * slab:(j + 1) * slab]
                across(j, p).start()
            return carry
        lax.fori_loop(0, pairs, one, 0)

    def near_late(p, carry):
        late(p).start()
        return carry

    def gram(p, carry):
        blocks = []
        for s in range(slots):
            name = dom_ref[s, q * pairs + p]
            local = lax.rem(name, chunks // split) * split
            for t in range(split):
                blocks.append(table[name // (chunks // split), local + t])
        stack = jnp.concatenate(blocks, axis=0)
        full = lax.dot_general(stack, stack, (((1,), (1,)), ((), ())), preferred_element_type=jnp.float32)
        d_own[p] = jnp.sum(jnp.where(row_of == col_of, full, 0.0), axis=0, keepdims=True)
        for d in range(n):
            part = full[d * slab:(d + 1) * slab]

            @pl.when(z == d)
            def _():
                out_ref[p] = part

        for end, below in ((0, True), (3, False)):
            near_cols, far_cols = (slice(0, half), slice(half, width))[::1 if below else -1]
            mid = 1 if below else 2

            @pl.when(z == end)
            def _():
                far_out[p] = full[:, far_cols].astype(far_out.dtype)
                late_send[p] = full[mid * slab:(mid + 1) * slab, near_cols].astype(late_send.dtype)
                to_mid(p).start()

            @pl.when(z == mid)
            def _():
                g_far[p] = full[far_cols]
                g_send[0, p] = full[end * slab:(end + 1) * slab].astype(g_send.dtype)
                near(p).start()
        return carry

    lax.fori_loop(0, pairs, gram, 0)

    def diag_copy(k):
        return remote(d_own, d_recv.at[k - 1], d_s.at[k - 1], d_r.at[k - 1], (lax.rem(z + k, n), q))

    for k in range(1, n):
        diag_copy(k).start()
    @pl.when(is_end)
    def _():
        lax.fori_loop(0, pairs, near_late, 0)

    for mid, below in ((1, True), (2, False)):
        @pl.when(z == mid)
        def _():
            combine(below)

    def add(p, carry):
        remote(g_send.at[0, p], g_recv.at[1, p], g_s.at[0, p], g_r.at[1, p], (mate, q)).wait_recv()
        total = out_ref[p] + g_recv[1, p].astype(jnp.float32)

        @pl.when(is_end)
        def _():
            near(p).wait_recv()
            out_ref[p] = total + g_recv[0, p].astype(jnp.float32)

        for mid, below in ((1, True), (2, False)):
            @pl.when(z == mid)
            def _():
                late(p).wait_recv()
                pieces = (late_recv[p], far_recv[p, mid * slab:(mid + 1) * slab])
                whole = jnp.concatenate(pieces if below else pieces[::-1], axis=1)
                out_ref[p] = total + whole.astype(jnp.float32)
        return carry

    lax.fori_loop(0, pairs, add, 0)
    for k in range(1, n):
        diag_copy(k).wait_recv()

    diag = d_own[...]
    for k in range(1, n):
        diag += d_recv[k - 1]
    diag_ref[...] = diag

    def drain_all(c, carry):
        swap(c).wait_send()
        drain(c)

        @pl.when(is_mid)
        def _():
            own(c).wait_send()
            relay(c).wait_send()
            half_fit(c).wait_send()
        return carry

    lax.fori_loop(0, chunks, drain_all, 0)
    for t in range(parts):
        @pl.when(is_end)
        def _():
            metric_part(t).wait_send()

        @pl.when(is_mid)
        def _():
            m_drain(t)

    def drain_gram(p, carry):
        @pl.when(is_end)
        def _():
            late(p).wait_send()
            to_mid(p).wait_send()

        @pl.when(is_mid)
        def _():
            near(p).wait_send()
            for j in range(2):
                across(j, p).wait_send()
        return carry

    lax.fori_loop(0, pairs, drain_gram, 0)
    for k in range(1, n):
        diag_copy(k).wait_send()


def close_kernel(rows, total_ref, diag_ref, cnt_ref, out_ref):
    pairs, slab, width = out_ref.shape
    slab_row = lax.broadcasted_iota(jnp.int32, (slab, width), 0) + lax.axis_index("aux") * slab
    slab_col = lax.broadcasted_iota(jnp.int32, (slab, width), 1)
    last = jnp.maximum(slab_row, slab_col)

    def close(p, carry):
        value = jnp.where(slab_row == slab_col, diag_ref[p], total_ref[p])
        out_ref[p] = jnp.where(last < cnt_ref[p] * rows, value, 0.0)
        return carry

    lax.fori_loop(0, pairs, close, 0)


def per_device(n, n_pair, b_three, metric, aux_map, domains, counts):
    rows_dev, aux_dev = b_three.shape
    blocks_dev, aux_blocks = aux_map.shape
    width_cw = rows_dev // blocks_dev
    pairs = counts.shape[0]
    slots = domains.shape[1]
    width = slots * width_cw
    slab = width // n
    split = 1
    chunks = blocks_dev * split
    chunk_rows = width_cw // split
    columns = metric.shape[1]
    chips = n_pair // 2
    box = n == 4 and n_pair == 8
    parts = n // 2 * aux_dev // (n_pair * chunk_rows)
    vmem = pl.BlockSpec(memory_space=pltpu.VMEM)
    smem = pl.BlockSpec(memory_space=pltpu.SMEM)
    dma = pltpu.SemaphoreType.DMA
    hbm = pl.BlockSpec(memory_space=pl.ANY)
    bf16 = jnp.bfloat16
    scratch = [
        pltpu.VMEM((chunks, chunk_rows, aux_dev), bf16),
        pltpu.VMEM((chunks, chunk_rows, aux_dev), bf16),
        pltpu.VMEM(metric.shape, bf16),
        dma((3,)),
        pltpu.VMEM((n, chunks, chunk_rows, aux_dev), bf16),
        pltpu.VMEM((n_pair, chunks, chunk_rows, columns), bf16),
    ]
    grams = [
        pltpu.VMEM((1 if box else n, pairs, slab, width), bf16),
        pltpu.VMEM((2 if box else n - 1, pairs, slab, width), bf16),
        pltpu.VMEM((pairs, 1, width), jnp.float32),
        pltpu.VMEM((n - 1, pairs, 1, width), jnp.float32),
    ]
    gram_sems = [dma((n - 1, pairs)), dma((n - 1, pairs)), dma((n - 1,)), dma((n - 1,))]
    if box:
        body = box_kernel
        scratch += [
            pltpu.VMEM((n_pair, parts, chunk_rows, columns), bf16),
            pltpu.VMEM((chunks, chunk_rows, columns), bf16),
            dma((chunks,)), dma((chunks,)), dma((2, chunks)), dma((2, chunks)),
            dma((chunks,)), dma((chunks,)), dma((parts,)), dma((parts,)),
        ]
        for count in (chunks, parts):
            scratch += [dma((k, count)) for k in (3, 3, 2, 2, 3, 3)]
        scratch += grams + gram_sems + [
            pltpu.VMEM((pairs, width // 2, width), jnp.float32),
            pltpu.VMEM((pairs, width, width // 2), bf16),
            pltpu.VMEM((pairs, width, width // 2), bf16),
            pltpu.VMEM((2, pairs, slab, width), bf16),
            pltpu.VMEM((pairs, slab, width // 2), bf16),
            pltpu.VMEM((pairs, slab, width // 2), bf16),
            dma((pairs,)), dma((pairs,)), dma((2, pairs)),
        ]
    else:
        body = line_kernel
        scratch += grams + [dma((n - 1, chunks)) for _ in range(4)] + [dma((chips, chunks)) for _ in range(4)] + gram_sems
    total, diag = pl.pallas_call(
        functools.partial(body, n, n_pair, split),
        out_shape=(jax.ShapeDtypeStruct((pairs, slab, width), jnp.float32),
                   jax.ShapeDtypeStruct((pairs, 1, width), jnp.float32)),
        in_specs=[hbm, hbm, vmem, smem],
        out_specs=(vmem, vmem),
        scratch_shapes=scratch,
        compiler_params=pltpu.CompilerParams(
            collective_id=0, has_side_effects=True, vmem_limit_bytes=60 * 1024 * 1024),
    )(b_three.reshape(chunks, chunk_rows, aux_dev), metric, aux_map, domains.T)
    return pl.pallas_call(
        functools.partial(close_kernel, width_cw),
        out_shape=jax.ShapeDtypeStruct((pairs, slab, width), jnp.float32),
        in_specs=[vmem, vmem, smem],
        out_specs=vmem,
    )(total, diag, counts)


def solution(mesh):
    return jax.shard_map(
        functools.partial(per_device, mesh.shape["aux"], mesh.shape["pair"]),
        mesh=mesh,
        in_specs=(P("pair", "aux"), P(None, "aux"), P("pair", "aux"), P(), P("pair")),
        out_specs=P("pair", "aux", None),
        check_vma=False,
    )
```

```python
import functools

import jax
import jax.numpy as jnp
from jax import lax
from jax.experimental import pallas as pl
from jax.experimental.pallas import tpu as pltpu
from jax.sharding import PartitionSpec as P

MESH = pl.DeviceIdType.MESH


def line_kernel(n, n_pair, split, b_hbm, metric_hbm, map_ref, dom_ref, out_ref, diag_ref,
           b_raw, b_ref, metric_ref, in_sem, b_all, table, g_send, g_recv, d_own, d_recv,
           r_s, r_r, l_s, l_r, p_s, p_r, f_s, f_r, g_s, g_r, d_s, d_r):
    chunks, rows, depth = b_hbm.shape
    pairs, slab, width = out_ref.shape
    slots = dom_ref.shape[0]
    chips = n_pair // 2
    z = lax.axis_index("aux")
    q = lax.axis_index("pair")
    core = lax.rem(q, 2)
    chip = q // 2
    partner = q + 1 - 2 * core
    has_right = z + 1 < n
    has_left = z > 0

    def chip_at(k):
        return lax.rem(chip + k + chips, chips) * 2 + core

    load_b = pltpu.make_async_copy(b_hbm.at[0], b_raw.at[0], in_sem.at[0])
    load_rest = pltpu.make_async_copy(b_hbm.at[1:], b_raw.at[1:], in_sem.at[2])
    load_metric = pltpu.make_async_copy(metric_hbm, metric_ref, in_sem.at[1])
    load_b.start()
    load_rest.start()
    load_metric.start()
    barrier = pltpu.get_barrier_semaphore()
    for near_z, there in ((z + 1, has_right), (z - 1, has_left)):
        @pl.when(there)
        def _():
            pl.semaphore_signal(barrier, inc=1, device_id=(near_z, q), device_id_type=MESH)
    for k in range(1, chips):
        pl.semaphore_signal(barrier, inc=1, device_id=(z, chip_at(k)), device_id_type=MESH)
    pl.semaphore_signal(barrier, inc=1, device_id=(z, partner), device_id_type=MESH)
    aux_blocks = map_ref.shape[1]
    spread_row = lax.broadcasted_iota(jnp.int32, (aux_blocks, depth), 0)
    spread_col = lax.broadcasted_iota(jnp.int32, (aux_blocks, depth), 1) // (depth // aux_blocks)
    keep = jnp.dot(map_ref[...].astype(jnp.float32), (spread_row == spread_col).astype(jnp.float32),
                   preferred_element_type=jnp.float32)
    def mask(c):
        b_ref[c] = (b_raw[c].astype(jnp.float32) * keep[c // split:c // split + 1, :]).astype(b_ref.dtype)
    load_b.wait()
    mask(0)
    pl.semaphore_wait(barrier, chips + has_right.astype(jnp.int32) + has_left.astype(jnp.int32))

    def remote(src, dst, send, recv, device):
        return pltpu.make_async_remote_copy(
            src_ref=src, dst_ref=dst, send_sem=send, recv_sem=recv, device_id=device, device_id_type=MESH)

    def along(h, c, right):
        step = 1 if right else -1
        origin = z - step * h
        send, recv = (r_s, r_r) if right else (l_s, l_r)
        src = b_ref.at[c] if h == 0 else b_all.at[origin, c]
        return remote(src, b_all.at[origin, c], send.at[h, c], recv.at[h, c], (z + step, q))

    def arrival(h, c, right):
        recv = r_r if right else l_r
        origin = z - 1 - h if right else z + 1 + h
        return remote(b_ref.at[c], b_all.at[origin, c], recv.at[h, c], recv.at[h, c], (z, partner))

    def own_chunk(c):
        for right in (True, False):
            @pl.when(has_right if right else has_left)
            def _():
                along(0, c, right).start()

    def relay(h, c):
        for right in (True, False):
            came = z - h >= 0 if right else z + h < n

            @pl.when(came)
            def _():
                arrival(h - 1, c, right).wait_recv()

                if h < n - 1:
                    @pl.when(has_right if right else has_left)
                    def _():
                        along(h, c, right).start()

    def spread(k, c):
        target = partner if k == 0 else chip_at(k)
        return remote(table.at[q, c], table.at[q, c], p_s.at[k, c], p_r.at[k, c], (z, target))

    def forward(k, c):
        origin = chip_at(-k)
        return remote(table.at[origin, c], table.at[origin, c], f_s.at[k, c], f_r.at[k, c], (z, partner))

    def fit(c):
        total = jnp.dot(b_ref[c], metric_ref[pl.ds(pl.multiple_of(z * depth, depth), depth), :],
                        preferred_element_type=jnp.float32)
        for k in range(1, n):
            origin = lax.rem(z + k, n)
            total += jnp.dot(b_all[origin, c],
                             metric_ref[pl.ds(pl.multiple_of(origin * depth, depth), depth), :],
                             preferred_element_type=jnp.float32)
        table[q, c] = total.astype(table.dtype)
        for k in list(range(1, chips)) + [0]:
            spread(k, c).start()

    def pass_on(c):
        for k in range(1, chips):
            spread_in = remote(table.at[chip_at(-k), c], table.at[chip_at(-k), c],
                               p_s.at[k, c], p_r.at[k, c], (z, partner))
            spread_in.wait_recv()
            forward(k, c).start()

    own_chunk(0)
    load_rest.wait()
    for c in range(1, chunks):
        mask(c)
    load_metric.wait()

    def stage(step, carry):
        @pl.when(step + 1 < chunks)
        def _():
            own_chunk(step + 1)
        for h in range(n - 1, 0, -1):
            @pl.when((step + 1 >= h) & (step + 1 - h < chunks))
            def _():
                relay(h, step + 1 - h)

        @pl.when((step + 2 >= n) & (step + 2 - n < chunks))
        def _():
            fit(step + 2 - n)

        @pl.when((step >= n) & (step - n < chunks))
        def _():
            pass_on(step - n)
        return carry

    lax.fori_loop(0, chunks + n, stage, 0)

    def finish(c, carry):
        remote(table.at[partner, c], table.at[partner, c], p_s.at[0, c], p_r.at[0, c],
               (z, partner)).wait_recv()
        for k in range(1, chips):
            origin = chip_at(-k) + 1 - 2 * core
            remote(table.at[origin, c], table.at[origin, c], f_s.at[k, c], f_r.at[k, c],
                   (z, partner)).wait_recv()
        return carry

    lax.fori_loop(0, chunks, finish, 0)

    row_of = lax.broadcasted_iota(jnp.int32, (width, width), 0)
    col_of = lax.broadcasted_iota(jnp.int32, (width, width), 1)

    def gram_copy(k, p):
        return remote(g_send.at[lax.rem(z + k, n), p], g_recv.at[k - 1, p],
                      g_s.at[k - 1, p], g_r.at[k - 1, p], (lax.rem(z + k, n), q))

    def gram(p, carry):
        blocks = []
        for s in range(slots):
            name = dom_ref[s, q * pairs + p]
            local = lax.rem(name, chunks // split) * split
            for t in range(split):
                blocks.append(table[name // (chunks // split), local + t])
        stack = jnp.concatenate(blocks, axis=0)
        full = lax.dot_general(stack, stack, (((1,), (1,)), ((), ())), preferred_element_type=jnp.float32)
        d_own[p] = jnp.sum(jnp.where(row_of == col_of, full, 0.0), axis=0, keepdims=True)
        for d in range(n):
            part = full[d * slab:(d + 1) * slab]

            @pl.when(z == d)
            def _():
                out_ref[p] = part

            @pl.when(z != d)
            def _():
                g_send[d, p] = part.astype(g_send.dtype)
        for k in range(1, n):
            gram_copy(k, p).start()
        return carry

    lax.fori_loop(0, pairs, gram, 0)

    def diag_copy(k):
        return remote(d_own, d_recv.at[k - 1], d_s.at[k - 1], d_r.at[k - 1], (lax.rem(z + k, n), q))

    for k in range(1, n):
        diag_copy(k).start()
    def add(p, carry):
        total = out_ref[p]
        for k in range(1, n):
            gram_copy(k, p).wait_recv()
            total += g_recv[k - 1, p].astype(jnp.float32)
        out_ref[p] = total
        return carry

    lax.fori_loop(0, pairs, add, 0)
    for k in range(1, n):
        diag_copy(k).wait_recv()

    diag = d_own[...]
    for k in range(1, n):
        diag += d_recv[k - 1]
    diag_ref[...] = diag

    def drain(c, carry):
        for right in (True, False):
            for h in range(n - 1):
                goes = (has_right & (z - h >= 0)) if right else (has_left & (z + h < n))

                @pl.when(goes)
                def _():
                    along(h, c, right).wait_send()
        for k in range(chips):
            spread(k, c).wait_send()
        for k in range(1, chips):
            forward(k, c).wait_send()
        return carry

    lax.fori_loop(0, chunks, drain, 0)

    def drain_gram(p, carry):
        for k in range(1, n):
            gram_copy(k, p).wait_send()
        return carry

    lax.fori_loop(0, pairs, drain_gram, 0)
    for k in range(1, n):
        diag_copy(k).wait_send()


def box_kernel(n, n_pair, split, b_hbm, metric_hbm, map_ref, dom_ref, out_ref, diag_ref,
               b_raw, metric_ref, in_sem, b_all, table, far_metric, fit_part,
               m_s, m_r, o_s, o_r, raw_s, raw_r, w_s, w_r, y_s, y_r,
               tp_s, tp_r, tt_s, tt_r, tf_s, tf_r, mp_s, mp_r, mt_s, mt_r, mf_s, mf_r,
               g_send, g_recv, d_own, d_recv, g_s, g_r, d_s, d_r,
               g_far, far_out, far_recv, far_send, late_send, late_recv, x_s, x_r, c_s):
    chunks, rows, depth = b_hbm.shape
    pairs, slab, width = out_ref.shape
    slots = dom_ref.shape[0]
    parts = far_metric.shape[1]
    z = lax.axis_index("aux")
    q = lax.axis_index("pair")
    core = lax.rem(q, 2)
    chip = q // 2
    flip = 1 - 2 * core
    partner = q + flip
    near_x = (chip + 1 - 2 * lax.rem(chip, 2)) * 2 + core
    near_y = lax.rem(chip + 2, 4) * 2 + core
    corner = (lax.rem(chip + 2, 4) + 1 - 2 * lax.rem(chip, 2)) * 2 + core
    mate = z + 1 - 2 * lax.rem(z, 2)
    other = n - 1 - z
    low = z < 2
    is_end = (z == 0) | (z == n - 1)
    is_mid = jnp.logical_not(is_end)

    load_b = pltpu.make_async_copy(b_hbm.at[0], b_raw.at[0], in_sem.at[0])
    load_rest = pltpu.make_async_copy(b_hbm.at[1:], b_raw.at[1:], in_sem.at[2])
    load_metric = pltpu.make_async_copy(metric_hbm, metric_ref, in_sem.at[1])
    load_b.start()
    load_rest.start()
    load_metric.start()
    barrier = pltpu.get_barrier_semaphore()
    for there in ((mate, q), (z, partner), (z, near_x), (z, near_y)):
        pl.semaphore_signal(barrier, inc=1, device_id=there, device_id_type=MESH)

    @pl.when(is_mid)
    def _():
        pl.semaphore_signal(barrier, inc=1, device_id=(other, q), device_id_type=MESH)

    aux_blocks = map_ref.shape[1]
    spread_row = lax.broadcasted_iota(jnp.int32, (aux_blocks, depth), 0)
    spread_col = lax.broadcasted_iota(jnp.int32, (aux_blocks, depth), 1) // (depth // aux_blocks)
    keep = jnp.dot(map_ref[...].astype(jnp.float32), (spread_row == spread_col).astype(jnp.float32),
                   preferred_element_type=jnp.float32)

    def mask(c):
        b_all[z, c] = (b_raw[c].astype(jnp.float32) * keep[c // split:c // split + 1, :]).astype(b_all.dtype)

    load_b.wait()
    mask(0)
    pl.semaphore_wait(barrier, 4 + is_mid.astype(jnp.int32))

    def remote(src, dst, send, recv, device):
        return pltpu.make_async_remote_copy(
            src_ref=src, dst_ref=dst, send_sem=send, recv_sem=recv, device_id=device, device_id_type=MESH)

    def swap(c, origin=None):
        at = b_all.at[z if origin is None else origin, c]
        return remote(at, at, m_s.at[c], m_r.at[c], (mate, q))

    def own(c, origin=None):
        at = b_all.at[z if origin is None else origin, c]
        return remote(at, at, o_s.at[0, c], o_r.at[0, c], (other, q))

    def relay(c, origin=None):
        at = b_all.at[mate if origin is None else origin, c]
        return remote(at, at, o_s.at[1, c], o_r.at[1, c], (other, q))

    def raw(k, c):
        at = b_all.at[other if k == 0 else n - 1 - mate, c]
        return remote(at, at, raw_s.at[k, c], raw_r.at[k, c], (mate, q))

    def raw_in(k, c):
        at = b_all.at[n - 1 - mate if k == 0 else other, c]
        return remote(at, at, raw_s.at[k, c], raw_r.at[k, c], (mate, q))

    def half_fit(c):
        return remote(fit_part.at[c], fit_part.at[c], w_s.at[c], w_r.at[c], (mate, q))

    far_first = jnp.where(z == 0, depth, 0)
    piece = parts * rows

    def metric_part(t):
        start = pl.multiple_of(far_first + q * piece + t * rows, rows)
        return remote(metric_ref.at[pl.ds(start, rows)], far_metric.at[q, t], y_s.at[t], y_r.at[t], (mate, q))

    def in_plane(buf, p_s, p_r, t_s, t_r, f_s, f_r):
        half = rows // 2

        def give(k, c):
            target = (partner, near_x, near_y)[k]
            return remote(buf.at[q, c], buf.at[q, c], p_s.at[k, c], p_r.at[k, c], (z, target))

        def turn(k, c):
            at = buf.at[(near_x, near_y)[k], c, pl.ds(k * half, half)]
            return remote(at, at, t_s.at[k, c], t_r.at[k, c], (z, (near_y, near_x)[k]))

        def forward(k, c):
            at = buf.at[(near_x, near_y, corner)[k], c]
            return remote(at, at, f_s.at[k, c], f_r.at[k, c], (z, partner))

        def share(c):
            for k in (1, 2, 0):
                give(k, c).start()

        def pass_on(c):
            for k in (0, 1):
                at = buf.at[(near_x, near_y)[k], c]
                remote(at, at, p_s.at[k + 1, c], p_r.at[k + 1, c], (z, partner)).wait_recv()
                turn(k, c).start()
                forward(k, c).start()

        def pass_corner(c):
            for k in (0, 1):
                at = buf.at[corner, c, pl.ds(k * half, half)]
                remote(at, at, t_s.at[k, c], t_r.at[k, c], (z, partner)).wait_recv()
            forward(2, c).start()

        def finish(c):
            at = buf.at[partner, c]
            remote(at, at, p_s.at[0, c], p_r.at[0, c], (z, partner)).wait_recv()
            for k in range(3):
                at = buf.at[(near_x, near_y, corner)[k] + flip, c]
                remote(at, at, f_s.at[k, c], f_r.at[k, c], (z, partner)).wait_recv()

        def drain(c):
            for k in range(3):
                give(k, c).wait_send()
                forward(k, c).wait_send()
            for k in range(2):
                turn(k, c).wait_send()

        return share, pass_on, pass_corner, finish, drain

    share, pass_on, pass_corner, finish, drain = in_plane(table, tp_s, tp_r, tt_s, tt_r, tf_s, tf_r)
    m_share, m_pass_on, m_pass_corner, m_finish, m_drain = in_plane(far_metric, mp_s, mp_r, mt_s, mt_r, mf_s, mf_r)

    whole = parts + 1

    def metric_rows(origin):
        return metric_ref[pl.ds(pl.multiple_of(origin * depth, depth), depth), :]

    def arrive(c):
        own(c, other).wait_recv()
        relay(c, n - 1 - mate).wait_recv()

    def fit(c):
        total = jnp.dot(b_all[z, c], metric_rows(z), preferred_element_type=jnp.float32)
        for k in range(1, n):
            origin = lax.rem(z + k, n)
            total += jnp.dot(b_all[origin, c], metric_rows(origin), preferred_element_type=jnp.float32)
        table[q, c] = total.astype(table.dtype)
        share(c)

    def fit_far(c):
        first = jnp.where(low, 1, 0)
        tiles = depth // rows // 2
        total = None
        for j in range(2 * (n - 1)):
            lhs = b_all[first + j // 2, c, :, (j % 2) * tiles * rows:(j % 2 + 1) * tiles * rows]
            rhs = jnp.concatenate([far_metric[u // parts, u % parts] for u in range(j * tiles, (j + 1) * tiles)], axis=0)
            term = jnp.dot(lhs, rhs, preferred_element_type=jnp.float32)
            total = term if total is None else total + term
        fit_part[c] = total.astype(fit_part.dtype)
        half_fit(c).start()

    def fit_end(c):
        total = jnp.dot(b_all[z, c], metric_rows(z), preferred_element_type=jnp.float32)
        half_fit(c).wait_recv()
        table[q, c] = (total + fit_part[c].astype(jnp.float32)).astype(table.dtype)
        share(c)

    @pl.when(is_mid)
    def _():
        own(0).start()

    swap(0).start()
    load_rest.wait()
    for c in range(1, chunks):
        mask(c)

        @pl.when(is_mid)
        def _():
            if c < 2:
                own(c).start()
            if c < whole:
                swap(c).start()

    load_metric.wait()

    @pl.when(is_end)
    def _():
        for c in range(1, chunks):
            if c <= parts:
                metric_part(c - 1).start()
            swap(c).start()

        def stage(c, carry):
            @pl.when(c < whole)
            def _():
                swap(c, mate).wait_recv()
                for k in (0, 1):
                    raw_in(k, c).wait_recv()
                fit(c)

            @pl.when((c >= whole) & (c < chunks))
            def _():
                fit_end(c)

            @pl.when((c >= 2) & (c < chunks + 2))
            def _():
                pass_on(c - 2)

            @pl.when(c >= 4)
            def _():
                pass_corner(c - 4)
            return carry

        lax.fori_loop(0, chunks + 4, stage, 0)

    @pl.when(is_mid)
    def _():
        def stage(s, carry):
            @pl.when((s >= 1) & (s <= parts))
            def _():
                t = s - 1
                at = far_metric.at[q, t]
                remote(at, at, y_s.at[t], y_r.at[t], (z, partner)).wait_recv()
                m_share(t)

            @pl.when(s < chunks)
            def _():
                swap(s, mate).wait_recv()
                relay(s).start()

            @pl.when(s + 2 < chunks)
            def _():
                own(s + 2).start()

            @pl.when((s >= 2) & (s < parts + 2))
            def _():
                m_pass_on(s - 2)

            @pl.when((s >= 3) & (s < parts + 3))
            def _():
                m_pass_corner(s - 3)

            c = s - 2
            inside = (c >= 0) & (c < chunks)

            @pl.when(inside)
            def _():
                own(c, other).wait_recv()
                relay(c, n - 1 - mate).wait_recv()

            @pl.when(inside & (c < whole))
            def _():
                for k in (0, 1):
                    raw(k, c).start()

            @pl.when(inside & (c > whole))
            def _():
                fit_far(c)

            @pl.when(inside)
            def _():
                fit(c)

            @pl.when(c == whole)
            def _():
                for t in range(parts):
                    m_finish(t)
                fit_far(c)

            @pl.when((s >= 4) & (s < chunks + 4))
            def _():
                pass_on(s - 4)

            @pl.when(s >= 6)
            def _():
                pass_corner(s - 6)
            return carry

        lax.fori_loop(0, chunks + 6, stage, 0)

    def finish_all(c, carry):
        finish(c)
        return carry

    lax.fori_loop(0, chunks, finish_all, 0)

    row_of = lax.broadcasted_iota(jnp.int32, (width, width), 0)
    col_of = lax.broadcasted_iota(jnp.int32, (width, width), 1)

    half = width // 2

    def near(p):
        return remote(g_send.at[0, p], g_recv.at[0, p], g_s.at[0, p], g_r.at[0, p], (mate, q))

    def late(p):
        return remote(late_send.at[p], late_recv.at[p], g_s.at[0, p], g_r.at[0, p], (mate, q))

    def to_mid(p):
        return remote(far_out.at[p], far_recv.at[p], x_s.at[p], x_r.at[p], (mate, q))

    def across(j, p):
        return remote(far_send.at[j, p], g_recv.at[1, p], c_s.at[j, p], g_r.at[1, p],
                      (jnp.where(z < 2, 2, 0) + j, q))

    def combine(below):
        def one(p, carry):
            to_mid(p).wait_recv()
            top = far_recv[p, 0:half].astype(jnp.float32)
            bottom = far_recv[p, half:width].astype(jnp.float32)
            parts = (top.T, bottom) if below else (top, bottom.T)
            value = (g_far[p] + jnp.concatenate(parts, axis=1)).astype(far_send.dtype)
            for j in ((1, 0) if below else (0, 1)):
                far_send[j, p] = value[j * slab:(j + 1) * slab]
                across(j, p).start()
            return carry
        lax.fori_loop(0, pairs, one, 0)

    def near_late(p, carry):
        late(p).start()
        return carry

    def gram(p, carry):
        blocks = []
        for s in range(slots):
            name = dom_ref[s, q * pairs + p]
            local = lax.rem(name, chunks // split) * split
            for t in range(split):
                blocks.append(table[name // (chunks // split), local + t])
        stack = jnp.concatenate(blocks, axis=0)
        full = lax.dot_general(stack, stack, (((1,), (1,)), ((), ())), preferred_element_type=jnp.float32)
        d_own[p] = jnp.sum(jnp.where(row_of == col_of, full, 0.0), axis=0, keepdims=True)
        for d in range(n):
            part = full[d * slab:(d + 1) * slab]

            @pl.when(z == d)
            def _():
                out_ref[p] = part

        for end, below in ((0, True), (3, False)):
            near_cols, far_cols = (slice(0, half), slice(half, width))[::1 if below else -1]
            mid = 1 if below else 2

            @pl.when(z == end)
            def _():
                far_out[p] = full[:, far_cols].astype(far_out.dtype)
                late_send[p] = full[mid * slab:(mid + 1) * slab, near_cols].astype(late_send.dtype)
                to_mid(p).start()

            @pl.when(z == mid)
            def _():
                g_far[p] = full[far_cols]
                g_send[0, p] = full[end * slab:(end + 1) * slab].astype(g_send.dtype)
                near(p).start()
        return carry

    lax.fori_loop(0, pairs, gram, 0)

    def diag_copy(k):
        return remote(d_own, d_recv.at[k - 1], d_s.at[k - 1], d_r.at[k - 1], (lax.rem(z + k, n), q))

    for k in range(1, n):
        diag_copy(k).start()
    @pl.when(is_end)
    def _():
        lax.fori_loop(0, pairs, near_late, 0)

    for mid, below in ((1, True), (2, False)):
        @pl.when(z == mid)
        def _():
            combine(below)

    def add(p, carry):
        remote(g_send.at[0, p], g_recv.at[1, p], g_s.at[0, p], g_r.at[1, p], (mate, q)).wait_recv()
        total = out_ref[p] + g_recv[1, p].astype(jnp.float32)

        @pl.when(is_end)
        def _():
            near(p).wait_recv()
            out_ref[p] = total + g_recv[0, p].astype(jnp.float32)

        for mid, below in ((1, True), (2, False)):
            @pl.when(z == mid)
            def _():
                late(p).wait_recv()
                pieces = (late_recv[p], far_recv[p, mid * slab:(mid + 1) * slab])
                whole = jnp.concatenate(pieces if below else pieces[::-1], axis=1)
                out_ref[p] = total + whole.astype(jnp.float32)
        return carry

    lax.fori_loop(0, pairs, add, 0)
    for k in range(1, n):
        diag_copy(k).wait_recv()

    diag = d_own[...]
    for k in range(1, n):
        diag += d_recv[k - 1]
    diag_ref[...] = diag

    def drain_all(c, carry):
        drain(c)

        @pl.when(is_end | (c < whole))
        def _():
            swap(c).wait_send()

        @pl.when(is_mid)
        def _():
            own(c).wait_send()
            relay(c).wait_send()

            @pl.when(c < whole)
            def _():
                for k in (0, 1):
                    raw(k, c).wait_send()

            @pl.when(c >= whole)
            def _():
                half_fit(c).wait_send()
        return carry

    lax.fori_loop(0, chunks, drain_all, 0)
    for t in range(parts):
        @pl.when(is_end)
        def _():
            metric_part(t).wait_send()

        @pl.when(is_mid)
        def _():
            m_drain(t)

    def drain_gram(p, carry):
        @pl.when(is_end)
        def _():
            late(p).wait_send()
            to_mid(p).wait_send()

        @pl.when(is_mid)
        def _():
            near(p).wait_send()
            for j in range(2):
                across(j, p).wait_send()
        return carry

    lax.fori_loop(0, pairs, drain_gram, 0)
    for k in range(1, n):
        diag_copy(k).wait_send()


def close_kernel(rows, total_ref, diag_ref, cnt_ref, out_ref):
    pairs, slab, width = out_ref.shape
    slab_row = lax.broadcasted_iota(jnp.int32, (slab, width), 0) + lax.axis_index("aux") * slab
    slab_col = lax.broadcasted_iota(jnp.int32, (slab, width), 1)
    last = jnp.maximum(slab_row, slab_col)

    def close(p, carry):
        value = jnp.where(slab_row == slab_col, diag_ref[p], total_ref[p])
        out_ref[p] = jnp.where(last < cnt_ref[p] * rows, value, 0.0)
        return carry

    lax.fori_loop(0, pairs, close, 0)


def per_device(n, n_pair, b_three, metric, aux_map, domains, counts):
    rows_dev, aux_dev = b_three.shape
    blocks_dev, aux_blocks = aux_map.shape
    width_cw = rows_dev // blocks_dev
    pairs = counts.shape[0]
    slots = domains.shape[1]
    width = slots * width_cw
    slab = width // n
    split = 1
    chunks = blocks_dev * split
    chunk_rows = width_cw // split
    columns = metric.shape[1]
    chips = n_pair // 2
    box = n == 4 and n_pair == 8
    parts = (n - 1) * aux_dev // (n_pair * chunk_rows)
    vmem = pl.BlockSpec(memory_space=pltpu.VMEM)
    smem = pl.BlockSpec(memory_space=pltpu.SMEM)
    dma = pltpu.SemaphoreType.DMA
    hbm = pl.BlockSpec(memory_space=pl.ANY)
    bf16 = jnp.bfloat16
    scratch = [pltpu.VMEM((chunks, chunk_rows, aux_dev), bf16) for _ in range(1 if box else 2)] + [
        pltpu.VMEM(metric.shape, bf16),
        dma((3,)),
        pltpu.VMEM((n, chunks, chunk_rows, aux_dev), bf16),
        pltpu.VMEM((n_pair, chunks, chunk_rows, columns), bf16),
    ]
    grams = [
        pltpu.VMEM((1 if box else n, pairs, slab, width), bf16),
        pltpu.VMEM((2 if box else n - 1, pairs, slab, width), bf16),
        pltpu.VMEM((pairs, 1, width), jnp.float32),
        pltpu.VMEM((n - 1, pairs, 1, width), jnp.float32),
    ]
    gram_sems = [dma((n - 1, pairs)), dma((n - 1, pairs)), dma((n - 1,)), dma((n - 1,))]
    if box:
        body = box_kernel
        scratch += [
            pltpu.VMEM((n_pair, parts, chunk_rows, columns), bf16),
            pltpu.VMEM((chunks, chunk_rows, columns), bf16),
            dma((chunks,)), dma((chunks,)), dma((2, chunks)), dma((2, chunks)), dma((2, chunks)), dma((2, chunks)),
            dma((chunks,)), dma((chunks,)), dma((parts,)), dma((parts,)),
        ]
        for count in (chunks, parts):
            scratch += [dma((k, count)) for k in (3, 3, 2, 2, 3, 3)]
        scratch += grams + gram_sems + [
            pltpu.VMEM((pairs, width // 2, width), jnp.float32),
            pltpu.VMEM((pairs, width, width // 2), bf16),
            pltpu.VMEM((pairs, width, width // 2), bf16),
            pltpu.VMEM((2, pairs, slab, width), bf16),
            pltpu.VMEM((pairs, slab, width // 2), bf16),
            pltpu.VMEM((pairs, slab, width // 2), bf16),
            dma((pairs,)), dma((pairs,)), dma((2, pairs)),
        ]
    else:
        body = line_kernel
        scratch += grams + [dma((n - 1, chunks)) for _ in range(4)] + [dma((chips, chunks)) for _ in range(4)] + gram_sems
    total, diag = pl.pallas_call(
        functools.partial(body, n, n_pair, split),
        out_shape=(jax.ShapeDtypeStruct((pairs, slab, width), jnp.float32),
                   jax.ShapeDtypeStruct((pairs, 1, width), jnp.float32)),
        in_specs=[hbm, hbm, vmem, smem],
        out_specs=(vmem, vmem),
        scratch_shapes=scratch,
        compiler_params=pltpu.CompilerParams(
            collective_id=0, has_side_effects=True, vmem_limit_bytes=60 * 1024 * 1024),
    )(b_three.reshape(chunks, chunk_rows, aux_dev), metric, aux_map, domains.T)
    return pl.pallas_call(
        functools.partial(close_kernel, width_cw),
        out_shape=jax.ShapeDtypeStruct((pairs, slab, width), jnp.float32),
        in_specs=[vmem, vmem, smem],
        out_specs=vmem,
    )(total, diag, counts)


def solution(mesh):
    return jax.shard_map(
        functools.partial(per_device, mesh.shape["aux"], mesh.shape["pair"]),
        mesh=mesh,
        in_specs=(P("pair", "aux"), P(None, "aux"), P("pair", "aux"), P(), P("pair")),
        out_specs=P("pair", "aux", None),
        check_vma=False,
    )
```

```python
import functools

import jax
import jax.numpy as jnp
from jax import lax
from jax.experimental import pallas as pl
from jax.experimental.pallas import tpu as pltpu
from jax.sharding import PartitionSpec as P

MESH = pl.DeviceIdType.MESH


def line_kernel(n, n_pair, split, b_hbm, metric_hbm, map_ref, dom_ref, out_ref, diag_ref,
           b_raw, b_ref, metric_ref, in_sem, b_all, table, g_send, g_recv, d_own, d_recv,
           r_s, r_r, l_s, l_r, p_s, p_r, f_s, f_r, g_s, g_r, d_s, d_r):
    chunks, rows, depth = b_hbm.shape
    pairs, slab, width = out_ref.shape
    slots = dom_ref.shape[0]
    chips = n_pair // 2
    z = lax.axis_index("aux")
    q = lax.axis_index("pair")
    core = lax.rem(q, 2)
    chip = q // 2
    partner = q + 1 - 2 * core
    has_right = z + 1 < n
    has_left = z > 0

    def chip_at(k):
        return lax.rem(chip + k + chips, chips) * 2 + core

    load_b = pltpu.make_async_copy(b_hbm.at[0], b_raw.at[0], in_sem.at[0])
    load_rest = pltpu.make_async_copy(b_hbm.at[1:], b_raw.at[1:], in_sem.at[2])
    load_metric = pltpu.make_async_copy(metric_hbm, metric_ref, in_sem.at[1])
    load_b.start()
    load_rest.start()
    load_metric.start()
    barrier = pltpu.get_barrier_semaphore()
    for near_z, there in ((z + 1, has_right), (z - 1, has_left)):
        @pl.when(there)
        def _():
            pl.semaphore_signal(barrier, inc=1, device_id=(near_z, q), device_id_type=MESH)
    for k in range(1, chips):
        pl.semaphore_signal(barrier, inc=1, device_id=(z, chip_at(k)), device_id_type=MESH)
    pl.semaphore_signal(barrier, inc=1, device_id=(z, partner), device_id_type=MESH)
    aux_blocks = map_ref.shape[1]
    spread_row = lax.broadcasted_iota(jnp.int32, (aux_blocks, depth), 0)
    spread_col = lax.broadcasted_iota(jnp.int32, (aux_blocks, depth), 1) // (depth // aux_blocks)
    keep = jnp.dot(map_ref[...].astype(jnp.float32), (spread_row == spread_col).astype(jnp.float32),
                   preferred_element_type=jnp.float32)
    def mask(c):
        b_ref[c] = (b_raw[c].astype(jnp.float32) * keep[c // split:c // split + 1, :]).astype(b_ref.dtype)
    load_b.wait()
    mask(0)
    pl.semaphore_wait(barrier, chips + has_right.astype(jnp.int32) + has_left.astype(jnp.int32))

    def remote(src, dst, send, recv, device):
        return pltpu.make_async_remote_copy(
            src_ref=src, dst_ref=dst, send_sem=send, recv_sem=recv, device_id=device, device_id_type=MESH)

    def along(h, c, right):
        step = 1 if right else -1
        origin = z - step * h
        send, recv = (r_s, r_r) if right else (l_s, l_r)
        src = b_ref.at[c] if h == 0 else b_all.at[origin, c]
        return remote(src, b_all.at[origin, c], send.at[h, c], recv.at[h, c], (z + step, q))

    def arrival(h, c, right):
        recv = r_r if right else l_r
        origin = z - 1 - h if right else z + 1 + h
        return remote(b_ref.at[c], b_all.at[origin, c], recv.at[h, c], recv.at[h, c], (z, partner))

    def own_chunk(c):
        for right in (True, False):
            @pl.when(has_right if right else has_left)
            def _():
                along(0, c, right).start()

    def relay(h, c):
        for right in (True, False):
            came = z - h >= 0 if right else z + h < n

            @pl.when(came)
            def _():
                arrival(h - 1, c, right).wait_recv()

                if h < n - 1:
                    @pl.when(has_right if right else has_left)
                    def _():
                        along(h, c, right).start()

    def spread(k, c):
        target = partner if k == 0 else chip_at(k)
        return remote(table.at[q, c], table.at[q, c], p_s.at[k, c], p_r.at[k, c], (z, target))

    def forward(k, c):
        origin = chip_at(-k)
        return remote(table.at[origin, c], table.at[origin, c], f_s.at[k, c], f_r.at[k, c], (z, partner))

    def fit(c):
        total = jnp.dot(b_ref[c], metric_ref[pl.ds(pl.multiple_of(z * depth, depth), depth), :],
                        preferred_element_type=jnp.float32)
        for k in range(1, n):
            origin = lax.rem(z + k, n)
            total += jnp.dot(b_all[origin, c],
                             metric_ref[pl.ds(pl.multiple_of(origin * depth, depth), depth), :],
                             preferred_element_type=jnp.float32)
        table[q, c] = total.astype(table.dtype)
        for k in list(range(1, chips)) + [0]:
            spread(k, c).start()

    def pass_on(c):
        for k in range(1, chips):
            spread_in = remote(table.at[chip_at(-k), c], table.at[chip_at(-k), c],
                               p_s.at[k, c], p_r.at[k, c], (z, partner))
            spread_in.wait_recv()
            forward(k, c).start()

    own_chunk(0)
    load_rest.wait()
    for c in range(1, chunks):
        mask(c)
    load_metric.wait()

    def stage(step, carry):
        @pl.when(step + 1 < chunks)
        def _():
            own_chunk(step + 1)
        for h in range(n - 1, 0, -1):
            @pl.when((step + 1 >= h) & (step + 1 - h < chunks))
            def _():
                relay(h, step + 1 - h)

        @pl.when((step + 2 >= n) & (step + 2 - n < chunks))
        def _():
            fit(step + 2 - n)

        @pl.when((step >= n) & (step - n < chunks))
        def _():
            pass_on(step - n)
        return carry

    lax.fori_loop(0, chunks + n, stage, 0)

    def finish(c, carry):
        remote(table.at[partner, c], table.at[partner, c], p_s.at[0, c], p_r.at[0, c],
               (z, partner)).wait_recv()
        for k in range(1, chips):
            origin = chip_at(-k) + 1 - 2 * core
            remote(table.at[origin, c], table.at[origin, c], f_s.at[k, c], f_r.at[k, c],
                   (z, partner)).wait_recv()
        return carry

    lax.fori_loop(0, chunks, finish, 0)

    row_of = lax.broadcasted_iota(jnp.int32, (width, width), 0)
    col_of = lax.broadcasted_iota(jnp.int32, (width, width), 1)

    def gram_copy(k, p):
        return remote(g_send.at[lax.rem(z + k, n), p], g_recv.at[k - 1, p],
                      g_s.at[k - 1, p], g_r.at[k - 1, p], (lax.rem(z + k, n), q))

    def gram(p, carry):
        blocks = []
        for s in range(slots):
            name = dom_ref[s, q * pairs + p]
            local = lax.rem(name, chunks // split) * split
            for t in range(split):
                blocks.append(table[name // (chunks // split), local + t])
        stack = jnp.concatenate(blocks, axis=0)
        full = lax.dot_general(stack, stack, (((1,), (1,)), ((), ())), preferred_element_type=jnp.float32)
        d_own[p] = jnp.sum(jnp.where(row_of == col_of, full, 0.0), axis=0, keepdims=True)
        for d in range(n):
            part = full[d * slab:(d + 1) * slab]

            @pl.when(z == d)
            def _():
                out_ref[p] = part

            @pl.when(z != d)
            def _():
                g_send[d, p] = part.astype(g_send.dtype)
        for k in range(1, n):
            gram_copy(k, p).start()
        return carry

    lax.fori_loop(0, pairs, gram, 0)

    def diag_copy(k):
        return remote(d_own, d_recv.at[k - 1], d_s.at[k - 1], d_r.at[k - 1], (lax.rem(z + k, n), q))

    for k in range(1, n):
        diag_copy(k).start()
    def add(p, carry):
        total = out_ref[p]
        for k in range(1, n):
            gram_copy(k, p).wait_recv()
            total += g_recv[k - 1, p].astype(jnp.float32)
        out_ref[p] = total
        return carry

    lax.fori_loop(0, pairs, add, 0)
    for k in range(1, n):
        diag_copy(k).wait_recv()

    diag = d_own[...]
    for k in range(1, n):
        diag += d_recv[k - 1]
    diag_ref[...] = diag

    def drain(c, carry):
        for right in (True, False):
            for h in range(n - 1):
                goes = (has_right & (z - h >= 0)) if right else (has_left & (z + h < n))

                @pl.when(goes)
                def _():
                    along(h, c, right).wait_send()
        for k in range(chips):
            spread(k, c).wait_send()
        for k in range(1, chips):
            forward(k, c).wait_send()
        return carry

    lax.fori_loop(0, chunks, drain, 0)

    def drain_gram(p, carry):
        for k in range(1, n):
            gram_copy(k, p).wait_send()
        return carry

    lax.fori_loop(0, pairs, drain_gram, 0)
    for k in range(1, n):
        diag_copy(k).wait_send()


def box_kernel(n, n_pair, split, b_hbm, metric_hbm, map_hbm, dom_hbm, out_hbm, diag_hbm,
               map_ref, dom_ref, out_ref, diag_ref, out_sem, b_raw, metric_ref, in_sem, b_all, table, far_metric, fit_part,
               m_s, m_r, o_s, o_r, raw_s, raw_r, w_s, w_r, y_s, y_r,
               tp_s, tp_r, tt_s, tt_r, tf_s, tf_r, mp_s, mp_r, mt_s, mt_r, mf_s, mf_r,
               g_send, g_recv, d_own, d_recv, g_s, g_r, d_s, d_r,
               g_far, far_out, far_recv, far_send, late_send, late_recv, x_s, x_r, c_s):
    chunks, rows, depth = b_hbm.shape
    pairs, slab, width = out_ref.shape
    slots = dom_ref.shape[0]
    parts = far_metric.shape[1]
    z = lax.axis_index("aux")
    q = lax.axis_index("pair")
    core = lax.rem(q, 2)
    chip = q // 2
    flip = 1 - 2 * core
    partner = q + flip
    near_x = (chip + 1 - 2 * lax.rem(chip, 2)) * 2 + core
    near_y = lax.rem(chip + 2, 4) * 2 + core
    corner = (lax.rem(chip + 2, 4) + 1 - 2 * lax.rem(chip, 2)) * 2 + core
    mate = z + 1 - 2 * lax.rem(z, 2)
    other = n - 1 - z
    low = z < 2
    is_end = (z == 0) | (z == n - 1)
    is_mid = jnp.logical_not(is_end)

    load_b = pltpu.make_async_copy(b_hbm.at[0], b_raw.at[0], in_sem.at[0])
    load_rest = pltpu.make_async_copy(b_hbm.at[1:], b_raw.at[1:], in_sem.at[2])
    load_metric = pltpu.make_async_copy(metric_hbm, metric_ref, in_sem.at[1])
    load_map = pltpu.make_async_copy(map_hbm, map_ref, in_sem.at[3])
    load_dom = pltpu.make_async_copy(dom_hbm, dom_ref, in_sem.at[4])
    load_map.start()
    load_b.start()
    load_rest.start()
    load_metric.start()
    load_dom.start()
    barrier = pltpu.get_barrier_semaphore()
    for there in ((mate, q), (z, partner), (z, near_x), (z, near_y)):
        pl.semaphore_signal(barrier, inc=1, device_id=there, device_id_type=MESH)

    @pl.when(is_mid)
    def _():
        pl.semaphore_signal(barrier, inc=1, device_id=(other, q), device_id_type=MESH)

    load_map.wait()
    aux_blocks = map_ref.shape[1]
    spread_row = lax.broadcasted_iota(jnp.int32, (aux_blocks, depth), 0)
    spread_col = lax.broadcasted_iota(jnp.int32, (aux_blocks, depth), 1) // (depth // aux_blocks)
    keep = jnp.dot(map_ref[...].astype(jnp.float32), (spread_row == spread_col).astype(jnp.float32),
                   preferred_element_type=jnp.float32)

    def mask(c):
        b_all[z, c] = (b_raw[c].astype(jnp.float32) * keep[c // split:c // split + 1, :]).astype(b_all.dtype)

    load_b.wait()
    mask(0)
    pl.semaphore_wait(barrier, 4 + is_mid.astype(jnp.int32))

    def remote(src, dst, send, recv, device):
        return pltpu.make_async_remote_copy(
            src_ref=src, dst_ref=dst, send_sem=send, recv_sem=recv, device_id=device, device_id_type=MESH)

    def swap(c, origin=None):
        at = b_all.at[z if origin is None else origin, c]
        return remote(at, at, m_s.at[c], m_r.at[c], (mate, q))

    def own(c, origin=None):
        at = b_all.at[z if origin is None else origin, c]
        return remote(at, at, o_s.at[0, c], o_r.at[0, c], (other, q))

    def relay(c, origin=None):
        at = b_all.at[mate if origin is None else origin, c]
        return remote(at, at, o_s.at[1, c], o_r.at[1, c], (other, q))

    def raw(k, c):
        at = b_all.at[other if k == 0 else n - 1 - mate, c]
        return remote(at, at, raw_s.at[k, c], raw_r.at[k, c], (mate, q))

    def raw_in(k, c):
        at = b_all.at[n - 1 - mate if k == 0 else other, c]
        return remote(at, at, raw_s.at[k, c], raw_r.at[k, c], (mate, q))

    def half_fit(c):
        return remote(fit_part.at[c], fit_part.at[c], w_s.at[c], w_r.at[c], (mate, q))

    far_first = jnp.where(z == 0, depth, 0)
    piece = parts * rows

    def metric_part(t):
        start = pl.multiple_of(far_first + q * piece + t * rows, rows)
        return remote(metric_ref.at[pl.ds(start, rows)], far_metric.at[q, t], y_s.at[t], y_r.at[t], (mate, q))

    def in_plane(buf, p_s, p_r, t_s, t_r, f_s, f_r):
        half = rows // 2

        def give(k, c):
            target = (partner, near_x, near_y)[k]
            return remote(buf.at[q, c], buf.at[q, c], p_s.at[k, c], p_r.at[k, c], (z, target))

        def turn(k, c):
            at = buf.at[(near_x, near_y)[k], c, pl.ds(k * half, half)]
            return remote(at, at, t_s.at[k, c], t_r.at[k, c], (z, (near_y, near_x)[k]))

        def forward(k, c):
            at = buf.at[(near_x, near_y, corner)[k], c]
            return remote(at, at, f_s.at[k, c], f_r.at[k, c], (z, partner))

        def share(c):
            for k in (1, 2, 0):
                give(k, c).start()

        def pass_on(c):
            for k in (0, 1):
                at = buf.at[(near_x, near_y)[k], c]
                remote(at, at, p_s.at[k + 1, c], p_r.at[k + 1, c], (z, partner)).wait_recv()
                turn(k, c).start()
                forward(k, c).start()

        def pass_corner(c):
            for k in (0, 1):
                at = buf.at[corner, c, pl.ds(k * half, half)]
                remote(at, at, t_s.at[k, c], t_r.at[k, c], (z, partner)).wait_recv()
            forward(2, c).start()

        def finish(c):
            at = buf.at[partner, c]
            remote(at, at, p_s.at[0, c], p_r.at[0, c], (z, partner)).wait_recv()
            for k in range(3):
                at = buf.at[(near_x, near_y, corner)[k] + flip, c]
                remote(at, at, f_s.at[k, c], f_r.at[k, c], (z, partner)).wait_recv()

        def drain(c):
            for k in range(3):
                give(k, c).wait_send()
                forward(k, c).wait_send()
            for k in range(2):
                turn(k, c).wait_send()

        return share, pass_on, pass_corner, finish, drain

    share, pass_on, pass_corner, finish, drain = in_plane(table, tp_s, tp_r, tt_s, tt_r, tf_s, tf_r)
    m_share, m_pass_on, m_pass_corner, m_finish, m_drain = in_plane(far_metric, mp_s, mp_r, mt_s, mt_r, mf_s, mf_r)

    whole = parts + 1

    def metric_rows(origin):
        return metric_ref[pl.ds(pl.multiple_of(origin * depth, depth), depth), :]

    def arrive(c):
        own(c, other).wait_recv()
        relay(c, n - 1 - mate).wait_recv()

    def fit(c):
        total = jnp.dot(b_all[z, c], metric_rows(z), preferred_element_type=jnp.float32)
        for k in range(1, n):
            origin = lax.rem(z + k, n)
            total += jnp.dot(b_all[origin, c], metric_rows(origin), preferred_element_type=jnp.float32)
        table[q, c] = total.astype(table.dtype)
        share(c)

    def fit_far(c):
        first = jnp.where(low, 1, 0)
        tiles = depth // rows // 2
        total = None
        for j in range(2 * (n - 1)):
            lhs = b_all[first + j // 2, c, :, (j % 2) * tiles * rows:(j % 2 + 1) * tiles * rows]
            rhs = jnp.concatenate([far_metric[u // parts, u % parts] for u in range(j * tiles, (j + 1) * tiles)], axis=0)
            term = jnp.dot(lhs, rhs, preferred_element_type=jnp.float32)
            total = term if total is None else total + term
        fit_part[c] = total.astype(fit_part.dtype)
        half_fit(c).start()

    def fit_end(c):
        total = jnp.dot(b_all[z, c], metric_rows(z), preferred_element_type=jnp.float32)
        half_fit(c).wait_recv()
        table[q, c] = (total + fit_part[c].astype(jnp.float32)).astype(table.dtype)
        share(c)

    @pl.when(is_mid)
    def _():
        own(0).start()

    swap(0).start()
    load_rest.wait()
    for c in range(1, chunks):
        mask(c)

        @pl.when(is_mid)
        def _():
            if c < 2:
                own(c).start()
            if c < whole:
                swap(c).start()

    load_metric.wait()

    @pl.when(is_end)
    def _():
        for c in range(1, chunks):
            if c <= parts:
                metric_part(c - 1).start()
            swap(c).start()

        def stage(c, carry):
            @pl.when(c < whole)
            def _():
                swap(c, mate).wait_recv()
                for k in (0, 1):
                    raw_in(k, c).wait_recv()
                fit(c)

            @pl.when((c >= whole) & (c < chunks))
            def _():
                fit_end(c)

            @pl.when((c >= 2) & (c < chunks + 2))
            def _():
                pass_on(c - 2)

            @pl.when(c >= 4)
            def _():
                pass_corner(c - 4)
            return carry

        lax.fori_loop(0, chunks + 4, stage, 0)

    @pl.when(is_mid)
    def _():
        def stage(s, carry):
            @pl.when((s >= 1) & (s <= parts))
            def _():
                t = s - 1
                at = far_metric.at[q, t]
                remote(at, at, y_s.at[t], y_r.at[t], (z, partner)).wait_recv()
                m_share(t)

            @pl.when(s < chunks)
            def _():
                swap(s, mate).wait_recv()
                relay(s).start()

            @pl.when(s + 2 < chunks)
            def _():
                own(s + 2).start()

            @pl.when((s >= 2) & (s < parts + 2))
            def _():
                m_pass_on(s - 2)

            @pl.when((s >= 3) & (s < parts + 3))
            def _():
                m_pass_corner(s - 3)

            c = s - 2
            inside = (c >= 0) & (c < chunks)

            @pl.when(inside)
            def _():
                own(c, other).wait_recv()
                relay(c, n - 1 - mate).wait_recv()

            @pl.when(inside & (c < whole))
            def _():
                for k in (0, 1):
                    raw(k, c).start()

            @pl.when(inside & (c > whole))
            def _():
                fit_far(c)

            @pl.when(inside)
            def _():
                fit(c)

            @pl.when(c == whole)
            def _():
                for t in range(parts):
                    m_finish(t)
                fit_far(c)

            @pl.when((s >= 4) & (s < chunks + 4))
            def _():
                pass_on(s - 4)

            @pl.when(s >= 6)
            def _():
                pass_corner(s - 6)
            return carry

        lax.fori_loop(0, chunks + 6, stage, 0)

    def finish_all(c, carry):
        finish(c)
        return carry

    load_dom.wait()
    lax.fori_loop(0, chunks, finish_all, 0)

    row_of = lax.broadcasted_iota(jnp.int32, (width, width), 0)
    col_of = lax.broadcasted_iota(jnp.int32, (width, width), 1)

    half = width // 2

    def near(p):
        return remote(g_send.at[0, p], g_recv.at[0, p], g_s.at[0, p], g_r.at[0, p], (mate, q))

    def late(p):
        return remote(late_send.at[p], late_recv.at[p], g_s.at[0, p], g_r.at[0, p], (mate, q))

    def to_mid(p):
        return remote(far_out.at[p], far_recv.at[p], x_s.at[p], x_r.at[p], (mate, q))

    def across(j, p):
        return remote(far_send.at[j, p], g_recv.at[1, p], c_s.at[j, p], g_r.at[1, p],
                      (jnp.where(z < 2, 2, 0) + j, q))

    def combine(below):
        def one(p, carry):
            to_mid(p).wait_recv()
            top = far_recv[p, 0:half].astype(jnp.float32)
            bottom = far_recv[p, half:width].astype(jnp.float32)
            parts = (top.T, bottom) if below else (top, bottom.T)
            value = (g_far[p] + jnp.concatenate(parts, axis=1)).astype(far_send.dtype)
            for j in ((1, 0) if below else (0, 1)):
                far_send[j, p] = value[j * slab:(j + 1) * slab]
                across(j, p).start()
            return carry
        lax.fori_loop(0, pairs, one, 0)

    def near_late(p, carry):
        late(p).start()
        return carry

    def gram(p, carry):
        blocks = []
        for s in range(slots):
            name = dom_ref[s, q * pairs + p]
            local = lax.rem(name, chunks // split) * split
            for t in range(split):
                blocks.append(table[name // (chunks // split), local + t])
        stack = jnp.concatenate(blocks, axis=0)
        full = lax.dot_general(stack, stack, (((1,), (1,)), ((), ())), preferred_element_type=jnp.float32)
        d_own[p] = jnp.sum(jnp.where(row_of == col_of, full, 0.0), axis=0, keepdims=True)
        for d in range(n):
            part = full[d * slab:(d + 1) * slab]

            @pl.when(z == d)
            def _():
                out_ref[p] = part

        for end, below in ((0, True), (3, False)):
            near_cols, far_cols = (slice(0, half), slice(half, width))[::1 if below else -1]
            mid = 1 if below else 2

            @pl.when(z == end)
            def _():
                far_out[p] = full[:, far_cols].astype(far_out.dtype)
                late_send[p] = full[mid * slab:(mid + 1) * slab, near_cols].astype(late_send.dtype)
                to_mid(p).start()

            @pl.when(z == mid)
            def _():
                g_far[p] = full[far_cols]
                g_send[0, p] = full[end * slab:(end + 1) * slab].astype(g_send.dtype)
                near(p).start()
        return carry

    lax.fori_loop(0, pairs, gram, 0)

    def diag_copy(k):
        return remote(d_own, d_recv.at[k - 1], d_s.at[k - 1], d_r.at[k - 1], (lax.rem(z + k, n), q))

    for k in range(1, n):
        diag_copy(k).start()
    @pl.when(is_end)
    def _():
        lax.fori_loop(0, pairs, near_late, 0)

    def drain_all(c, carry):
        drain(c)

        @pl.when(is_end | (c < whole))
        def _():
            swap(c).wait_send()

        @pl.when(is_mid)
        def _():
            own(c).wait_send()
            relay(c).wait_send()

            @pl.when(c < whole)
            def _():
                for k in (0, 1):
                    raw(k, c).wait_send()

            @pl.when(c >= whole)
            def _():
                half_fit(c).wait_send()
        return carry

    lax.fori_loop(0, chunks, drain_all, 0)
    for t in range(parts):
        @pl.when(is_end)
        def _():
            metric_part(t).wait_send()

        @pl.when(is_mid)
        def _():
            m_drain(t)

    for mid, below in ((1, True), (2, False)):
        @pl.when(z == mid)
        def _():
            combine(below)

    def leave(p):
        return pltpu.make_async_copy(out_ref.at[p], out_hbm.at[p], out_sem.at[p])

    leave_diag = pltpu.make_async_copy(diag_ref, diag_hbm, in_sem.at[3])
    for k in range(1, n):
        diag_copy(k).wait_recv()

    diag = d_own[...]
    for k in range(1, n):
        diag += d_recv[k - 1]
    diag_ref[...] = diag
    leave_diag.start()

    def add(p, carry):
        remote(g_send.at[0, p], g_recv.at[1, p], g_s.at[0, p], g_r.at[1, p], (mate, q)).wait_recv()
        total = out_ref[p] + g_recv[1, p].astype(jnp.float32)

        @pl.when(is_end)
        def _():
            near(p).wait_recv()
            out_ref[p] = total + g_recv[0, p].astype(jnp.float32)

        for mid, below in ((1, True), (2, False)):
            @pl.when(z == mid)
            def _():
                late(p).wait_recv()
                pieces = (late_recv[p], far_recv[p, mid * slab:(mid + 1) * slab])
                whole = jnp.concatenate(pieces if below else pieces[::-1], axis=1)
                out_ref[p] = total + whole.astype(jnp.float32)

        leave(p).start()
        return carry

    lax.fori_loop(0, pairs, add, 0)

    def drain_gram(p, carry):
        leave(p).wait()

        @pl.when(is_end)
        def _():
            late(p).wait_send()
            to_mid(p).wait_send()

        @pl.when(is_mid)
        def _():
            near(p).wait_send()
            for j in range(2):
                across(j, p).wait_send()
        return carry

    lax.fori_loop(0, pairs, drain_gram, 0)
    leave_diag.wait()
    for k in range(1, n):
        diag_copy(k).wait_send()


def close_kernel(rows, total_ref, diag_ref, cnt_ref, out_ref):
    pairs, slab, width = out_ref.shape
    slab_row = lax.broadcasted_iota(jnp.int32, (slab, width), 0) + lax.axis_index("aux") * slab
    slab_col = lax.broadcasted_iota(jnp.int32, (slab, width), 1)
    last = jnp.maximum(slab_row, slab_col)

    def close(p, carry):
        value = jnp.where(slab_row == slab_col, diag_ref[p], total_ref[p])
        out_ref[p] = jnp.where(last < cnt_ref[p] * rows, value, 0.0)
        return carry

    lax.fori_loop(0, pairs, close, 0)


def per_device(n, n_pair, b_three, metric, aux_map, domains, counts):
    rows_dev, aux_dev = b_three.shape
    blocks_dev, aux_blocks = aux_map.shape
    width_cw = rows_dev // blocks_dev
    pairs = counts.shape[0]
    slots = domains.shape[1]
    width = slots * width_cw
    slab = width // n
    split = 1
    chunks = blocks_dev * split
    chunk_rows = width_cw // split
    columns = metric.shape[1]
    chips = n_pair // 2
    box = n == 4 and n_pair == 8
    parts = (n - 1) * aux_dev // (n_pair * chunk_rows)
    vmem = pl.BlockSpec(memory_space=pltpu.VMEM)
    smem = pl.BlockSpec(memory_space=pltpu.SMEM)
    dma = pltpu.SemaphoreType.DMA
    hbm = pl.BlockSpec(memory_space=pl.ANY)
    bf16 = jnp.bfloat16
    scratch = [pltpu.VMEM((chunks, chunk_rows, aux_dev), bf16) for _ in range(1 if box else 2)] + [
        pltpu.VMEM(metric.shape, bf16),
        dma((5,)),
        pltpu.VMEM((n, chunks, chunk_rows, aux_dev), bf16),
        pltpu.VMEM((n_pair, chunks, chunk_rows, columns), bf16),
    ]
    grams = [
        pltpu.VMEM((1 if box else n, pairs, slab, width), bf16),
        pltpu.VMEM((2 if box else n - 1, pairs, slab, width), bf16),
        pltpu.VMEM((pairs, 1, width), jnp.float32),
        pltpu.VMEM((n - 1, pairs, 1, width), jnp.float32),
    ]
    gram_sems = [dma((n - 1, pairs)), dma((n - 1, pairs)), dma((n - 1,)), dma((n - 1,))]
    specs, outs = [hbm, hbm, vmem, smem], (vmem, vmem)
    if box:
        body = box_kernel
        specs, outs = [hbm] * 4, (hbm, hbm)
        scratch = [
            pltpu.VMEM(aux_map.shape, jnp.int32),
            pltpu.SMEM((slots, domains.shape[0]), jnp.int32),
            pltpu.VMEM((pairs, slab, width), jnp.float32),
            pltpu.VMEM((pairs, 1, width), jnp.float32),
            dma((pairs,)),
        ] + scratch
        scratch += [
            pltpu.VMEM((n_pair, parts, chunk_rows, columns), bf16),
            pltpu.VMEM((chunks, chunk_rows, columns), bf16),
            dma((chunks,)), dma((chunks,)), dma((2, chunks)), dma((2, chunks)), dma((2, chunks)), dma((2, chunks)),
            dma((chunks,)), dma((chunks,)), dma((parts,)), dma((parts,)),
        ]
        for count in (chunks, parts):
            scratch += [dma((k, count)) for k in (3, 3, 2, 2, 3, 3)]
        scratch += grams + gram_sems + [
            pltpu.VMEM((pairs, width // 2, width), jnp.float32),
            pltpu.VMEM((pairs, width, width // 2), bf16),
            pltpu.VMEM((pairs, width, width // 2), bf16),
            pltpu.VMEM((2, pairs, slab, width), bf16),
            pltpu.VMEM((pairs, slab, width // 2), bf16),
            pltpu.VMEM((pairs, slab, width // 2), bf16),
            dma((pairs,)), dma((pairs,)), dma((2, pairs)),
        ]
    else:
        body = line_kernel
        scratch += grams + [dma((n - 1, chunks)) for _ in range(4)] + [dma((chips, chunks)) for _ in range(4)] + gram_sems
    total, diag = pl.pallas_call(
        functools.partial(body, n, n_pair, split),
        out_shape=(jax.ShapeDtypeStruct((pairs, slab, width), jnp.float32),
                   jax.ShapeDtypeStruct((pairs, 1, width), jnp.float32)),
        in_specs=specs,
        out_specs=outs,
        scratch_shapes=scratch,
        compiler_params=pltpu.CompilerParams(
            collective_id=0, has_side_effects=True, vmem_limit_bytes=60 * 1024 * 1024),
    )(b_three.reshape(chunks, chunk_rows, aux_dev), metric, aux_map, domains.T)
    return pl.pallas_call(
        functools.partial(close_kernel, width_cw),
        out_shape=jax.ShapeDtypeStruct((pairs, slab, width), jnp.float32),
        in_specs=[vmem, vmem, smem],
        out_specs=vmem,
    )(total, diag, counts)


def solution(mesh):
    return jax.shard_map(
        functools.partial(per_device, mesh.shape["aux"], mesh.shape["pair"]),
        mesh=mesh,
        in_specs=(P("pair", "aux"), P(None, "aux"), P("pair", "aux"), P(), P("pair")),
        out_specs=P("pair", "aux", None),
        check_vma=False,
    )
```

```python
import functools

import jax
import jax.numpy as jnp
from jax import lax
from jax.experimental import pallas as pl
from jax.experimental.pallas import tpu as pltpu
from jax.sharding import PartitionSpec as P

MESH = pl.DeviceIdType.MESH


def line_kernel(n, n_pair, split, b_hbm, metric_hbm, map_ref, dom_ref, out_ref, diag_ref,
           b_raw, b_ref, metric_ref, in_sem, b_all, table, g_send, g_recv, d_own, d_recv,
           r_s, r_r, l_s, l_r, p_s, p_r, f_s, f_r, g_s, g_r, d_s, d_r):
    chunks, rows, depth = b_hbm.shape
    pairs, slab, width = out_ref.shape
    slots = dom_ref.shape[0]
    chips = n_pair // 2
    z = lax.axis_index("aux")
    q = lax.axis_index("pair")
    core = lax.rem(q, 2)
    chip = q // 2
    partner = q + 1 - 2 * core
    has_right = z + 1 < n
    has_left = z > 0

    def chip_at(k):
        return lax.rem(chip + k + chips, chips) * 2 + core

    load_b = pltpu.make_async_copy(b_hbm.at[0], b_raw.at[0], in_sem.at[0])
    load_rest = pltpu.make_async_copy(b_hbm.at[1:], b_raw.at[1:], in_sem.at[2])
    load_metric = pltpu.make_async_copy(metric_hbm, metric_ref, in_sem.at[1])
    load_b.start()
    load_rest.start()
    load_metric.start()
    barrier = pltpu.get_barrier_semaphore()
    for near_z, there in ((z + 1, has_right), (z - 1, has_left)):
        @pl.when(there)
        def _():
            pl.semaphore_signal(barrier, inc=1, device_id=(near_z, q), device_id_type=MESH)
    for k in range(1, chips):
        pl.semaphore_signal(barrier, inc=1, device_id=(z, chip_at(k)), device_id_type=MESH)
    pl.semaphore_signal(barrier, inc=1, device_id=(z, partner), device_id_type=MESH)
    aux_blocks = map_ref.shape[1]
    spread_row = lax.broadcasted_iota(jnp.int32, (aux_blocks, depth), 0)
    spread_col = lax.broadcasted_iota(jnp.int32, (aux_blocks, depth), 1) // (depth // aux_blocks)
    keep = jnp.dot(map_ref[...].astype(jnp.float32), (spread_row == spread_col).astype(jnp.float32),
                   preferred_element_type=jnp.float32)
    def mask(c):
        b_ref[c] = (b_raw[c].astype(jnp.float32) * keep[c // split:c // split + 1, :]).astype(b_ref.dtype)
    load_b.wait()
    mask(0)
    pl.semaphore_wait(barrier, chips + has_right.astype(jnp.int32) + has_left.astype(jnp.int32))

    def remote(src, dst, send, recv, device):
        return pltpu.make_async_remote_copy(
            src_ref=src, dst_ref=dst, send_sem=send, recv_sem=recv, device_id=device, device_id_type=MESH)

    def along(h, c, right):
        step = 1 if right else -1
        origin = z - step * h
        send, recv = (r_s, r_r) if right else (l_s, l_r)
        src = b_ref.at[c] if h == 0 else b_all.at[origin, c]
        return remote(src, b_all.at[origin, c], send.at[h, c], recv.at[h, c], (z + step, q))

    def arrival(h, c, right):
        recv = r_r if right else l_r
        origin = z - 1 - h if right else z + 1 + h
        return remote(b_ref.at[c], b_all.at[origin, c], recv.at[h, c], recv.at[h, c], (z, partner))

    def own_chunk(c):
        for right in (True, False):
            @pl.when(has_right if right else has_left)
            def _():
                along(0, c, right).start()

    def relay(h, c):
        for right in (True, False):
            came = z - h >= 0 if right else z + h < n

            @pl.when(came)
            def _():
                arrival(h - 1, c, right).wait_recv()

                if h < n - 1:
                    @pl.when(has_right if right else has_left)
                    def _():
                        along(h, c, right).start()

    def spread(k, c):
        target = partner if k == 0 else chip_at(k)
        return remote(table.at[q, c], table.at[q, c], p_s.at[k, c], p_r.at[k, c], (z, target))

    def forward(k, c):
        origin = chip_at(-k)
        return remote(table.at[origin, c], table.at[origin, c], f_s.at[k, c], f_r.at[k, c], (z, partner))

    def fit(c):
        total = jnp.dot(b_ref[c], metric_ref[pl.ds(pl.multiple_of(z * depth, depth), depth), :],
                        preferred_element_type=jnp.float32)
        for k in range(1, n):
            origin = lax.rem(z + k, n)
            total += jnp.dot(b_all[origin, c],
                             metric_ref[pl.ds(pl.multiple_of(origin * depth, depth), depth), :],
                             preferred_element_type=jnp.float32)
        table[q, c] = total.astype(table.dtype)
        for k in list(range(1, chips)) + [0]:
            spread(k, c).start()

    def pass_on(c):
        for k in range(1, chips):
            spread_in = remote(table.at[chip_at(-k), c], table.at[chip_at(-k), c],
                               p_s.at[k, c], p_r.at[k, c], (z, partner))
            spread_in.wait_recv()
            forward(k, c).start()

    own_chunk(0)
    load_rest.wait()
    for c in range(1, chunks):
        mask(c)
    load_metric.wait()

    def stage(step, carry):
        @pl.when(step + 1 < chunks)
        def _():
            own_chunk(step + 1)
        for h in range(n - 1, 0, -1):
            @pl.when((step + 1 >= h) & (step + 1 - h < chunks))
            def _():
                relay(h, step + 1 - h)

        @pl.when((step + 2 >= n) & (step + 2 - n < chunks))
        def _():
            fit(step + 2 - n)

        @pl.when((step >= n) & (step - n < chunks))
        def _():
            pass_on(step - n)
        return carry

    lax.fori_loop(0, chunks + n, stage, 0)

    def finish(c, carry):
        remote(table.at[partner, c], table.at[partner, c], p_s.at[0, c], p_r.at[0, c],
               (z, partner)).wait_recv()
        for k in range(1, chips):
            origin = chip_at(-k) + 1 - 2 * core
            remote(table.at[origin, c], table.at[origin, c], f_s.at[k, c], f_r.at[k, c],
                   (z, partner)).wait_recv()
        return carry

    lax.fori_loop(0, chunks, finish, 0)

    row_of = lax.broadcasted_iota(jnp.int32, (width, width), 0)
    col_of = lax.broadcasted_iota(jnp.int32, (width, width), 1)

    def gram_copy(k, p):
        return remote(g_send.at[lax.rem(z + k, n), p], g_recv.at[k - 1, p],
                      g_s.at[k - 1, p], g_r.at[k - 1, p], (lax.rem(z + k, n), q))

    def gram(p, carry):
        blocks = []
        for s in range(slots):
            name = dom_ref[s, q * pairs + p]
            local = lax.rem(name, chunks // split) * split
            for t in range(split):
                blocks.append(table[name // (chunks // split), local + t])
        stack = jnp.concatenate(blocks, axis=0)
        full = lax.dot_general(stack, stack, (((1,), (1,)), ((), ())), preferred_element_type=jnp.float32)
        d_own[p] = jnp.sum(jnp.where(row_of == col_of, full, 0.0), axis=0, keepdims=True)
        for d in range(n):
            part = full[d * slab:(d + 1) * slab]

            @pl.when(z == d)
            def _():
                out_ref[p] = part

            @pl.when(z != d)
            def _():
                g_send[d, p] = part.astype(g_send.dtype)
        for k in range(1, n):
            gram_copy(k, p).start()
        return carry

    lax.fori_loop(0, pairs, gram, 0)

    def diag_copy(k):
        return remote(d_own, d_recv.at[k - 1], d_s.at[k - 1], d_r.at[k - 1], (lax.rem(z + k, n), q))

    for k in range(1, n):
        diag_copy(k).start()
    def add(p, carry):
        total = out_ref[p]
        for k in range(1, n):
            gram_copy(k, p).wait_recv()
            total += g_recv[k - 1, p].astype(jnp.float32)
        out_ref[p] = total
        return carry

    lax.fori_loop(0, pairs, add, 0)
    for k in range(1, n):
        diag_copy(k).wait_recv()

    diag = d_own[...]
    for k in range(1, n):
        diag += d_recv[k - 1]
    diag_ref[...] = diag

    def drain(c, carry):
        for right in (True, False):
            for h in range(n - 1):
                goes = (has_right & (z - h >= 0)) if right else (has_left & (z + h < n))

                @pl.when(goes)
                def _():
                    along(h, c, right).wait_send()
        for k in range(chips):
            spread(k, c).wait_send()
        for k in range(1, chips):
            forward(k, c).wait_send()
        return carry

    lax.fori_loop(0, chunks, drain, 0)

    def drain_gram(p, carry):
        for k in range(1, n):
            gram_copy(k, p).wait_send()
        return carry

    lax.fori_loop(0, pairs, drain_gram, 0)
    for k in range(1, n):
        diag_copy(k).wait_send()


def box_kernel(n, n_pair, split, b_hbm, metric_hbm, map_hbm, dom_hbm, out_hbm, diag_hbm,
               map_ref, dom_ref, out_ref, diag_ref, out_sem, b_raw, metric_ref, in_sem, b_all, table, far_metric, fit_part,
               m_s, m_r, o_s, o_r, raw_s, raw_r, w_s, w_r, y_s, y_r,
               tp_s, tp_r, tt_s, tt_r, tf_s, tf_r, mp_s, mp_r, mt_s, mt_r, mf_s, mf_r,
               g_send, g_recv, d_own, d_recv, g_s, g_r, d_s, d_r,
               g_far, far_out, far_recv, far_send, v_recv, t_recv, late_send, late_recv, x_s, x_r, c_s):
    chunks, rows, depth = b_hbm.shape
    pairs, slab, width = out_ref.shape
    slots = dom_ref.shape[0]
    parts = far_metric.shape[1]
    z = lax.axis_index("aux")
    q = lax.axis_index("pair")
    core = lax.rem(q, 2)
    chip = q // 2
    flip = 1 - 2 * core
    partner = q + flip
    near_x = (chip + 1 - 2 * lax.rem(chip, 2)) * 2 + core
    near_y = lax.rem(chip + 2, 4) * 2 + core
    corner = (lax.rem(chip + 2, 4) + 1 - 2 * lax.rem(chip, 2)) * 2 + core
    mate = z + 1 - 2 * lax.rem(z, 2)
    other = n - 1 - z
    low = z < 2
    is_end = (z == 0) | (z == n - 1)
    is_mid = jnp.logical_not(is_end)

    load_b = pltpu.make_async_copy(b_hbm.at[0], b_raw.at[0], in_sem.at[0])
    load_rest = pltpu.make_async_copy(b_hbm.at[1:], b_raw.at[1:], in_sem.at[2])
    load_metric = pltpu.make_async_copy(metric_hbm, metric_ref, in_sem.at[1])
    load_map = pltpu.make_async_copy(map_hbm, map_ref, in_sem.at[3])
    load_dom = pltpu.make_async_copy(dom_hbm, dom_ref, in_sem.at[4])
    load_map.start()
    load_b.start()
    load_rest.start()
    load_metric.start()
    load_dom.start()
    barrier = pltpu.get_barrier_semaphore()
    for there in ((mate, q), (z, partner), (z, near_x), (z, near_y)):
        pl.semaphore_signal(barrier, inc=1, device_id=there, device_id_type=MESH)

    @pl.when(is_mid)
    def _():
        pl.semaphore_signal(barrier, inc=1, device_id=(other, q), device_id_type=MESH)

    load_map.wait()
    aux_blocks = map_ref.shape[1]
    spread_row = lax.broadcasted_iota(jnp.int32, (aux_blocks, depth), 0)
    spread_col = lax.broadcasted_iota(jnp.int32, (aux_blocks, depth), 1) // (depth // aux_blocks)
    keep = jnp.dot(map_ref[...].astype(jnp.float32), (spread_row == spread_col).astype(jnp.float32),
                   preferred_element_type=jnp.float32)

    def mask(c):
        b_all[z, c] = (b_raw[c].astype(jnp.float32) * keep[c // split:c // split + 1, :]).astype(b_all.dtype)

    load_b.wait()
    mask(0)
    pl.semaphore_wait(barrier, 4 + is_mid.astype(jnp.int32))

    def remote(src, dst, send, recv, device):
        return pltpu.make_async_remote_copy(
            src_ref=src, dst_ref=dst, send_sem=send, recv_sem=recv, device_id=device, device_id_type=MESH)

    def swap(c, origin=None):
        at = b_all.at[z if origin is None else origin, c]
        return remote(at, at, m_s.at[c], m_r.at[c], (mate, q))

    def own(c, origin=None):
        at = b_all.at[z if origin is None else origin, c]
        return remote(at, at, o_s.at[0, c], o_r.at[0, c], (other, q))

    def relay(c, origin=None):
        at = b_all.at[mate if origin is None else origin, c]
        return remote(at, at, o_s.at[1, c], o_r.at[1, c], (other, q))

    def raw(k, c):
        at = b_all.at[other if k == 0 else n - 1 - mate, c]
        return remote(at, at, raw_s.at[k, c], raw_r.at[k, c], (mate, q))

    def raw_in(k, c):
        at = b_all.at[n - 1 - mate if k == 0 else other, c]
        return remote(at, at, raw_s.at[k, c], raw_r.at[k, c], (mate, q))

    def half_fit(c):
        return remote(fit_part.at[c], fit_part.at[c], w_s.at[c], w_r.at[c], (mate, q))

    far_first = jnp.where(z == 0, depth, 0)
    piece = parts * rows

    def metric_part(t):
        start = pl.multiple_of(far_first + q * piece + t * rows, rows)
        return remote(metric_ref.at[pl.ds(start, rows)], far_metric.at[q, t], y_s.at[t], y_r.at[t], (mate, q))

    def in_plane(buf, p_s, p_r, t_s, t_r, f_s, f_r):
        half = rows // 2

        def give(k, c):
            target = (partner, near_x, near_y)[k]
            return remote(buf.at[q, c], buf.at[q, c], p_s.at[k, c], p_r.at[k, c], (z, target))

        def turn(k, c):
            at = buf.at[(near_x, near_y)[k], c, pl.ds(k * half, half)]
            return remote(at, at, t_s.at[k, c], t_r.at[k, c], (z, (near_y, near_x)[k]))

        def forward(k, c):
            at = buf.at[(near_x, near_y, corner)[k], c]
            return remote(at, at, f_s.at[k, c], f_r.at[k, c], (z, partner))

        def share(c):
            for k in (1, 2, 0):
                give(k, c).start()

        def pass_on(c):
            for k in (0, 1):
                at = buf.at[(near_x, near_y)[k], c]
                remote(at, at, p_s.at[k + 1, c], p_r.at[k + 1, c], (z, partner)).wait_recv()
                turn(k, c).start()
                forward(k, c).start()

        def pass_corner(c):
            for k in (0, 1):
                at = buf.at[corner, c, pl.ds(k * half, half)]
                remote(at, at, t_s.at[k, c], t_r.at[k, c], (z, partner)).wait_recv()
            forward(2, c).start()

        def finish(c):
            at = buf.at[partner, c]
            remote(at, at, p_s.at[0, c], p_r.at[0, c], (z, partner)).wait_recv()
            for k in range(3):
                at = buf.at[(near_x, near_y, corner)[k] + flip, c]
                remote(at, at, f_s.at[k, c], f_r.at[k, c], (z, partner)).wait_recv()

        def drain(c):
            for k in range(3):
                give(k, c).wait_send()
                forward(k, c).wait_send()
            for k in range(2):
                turn(k, c).wait_send()

        return share, pass_on, pass_corner, finish, drain

    share, pass_on, pass_corner, finish, drain = in_plane(table, tp_s, tp_r, tt_s, tt_r, tf_s, tf_r)
    m_share, m_pass_on, m_pass_corner, m_finish, m_drain = in_plane(far_metric, mp_s, mp_r, mt_s, mt_r, mf_s, mf_r)

    whole = parts + 1

    def metric_rows(origin):
        return metric_ref[pl.ds(pl.multiple_of(origin * depth, depth), depth), :]

    def arrive(c):
        own(c, other).wait_recv()
        relay(c, n - 1 - mate).wait_recv()

    def fit(c):
        total = jnp.dot(b_all[z, c], metric_rows(z), preferred_element_type=jnp.float32)
        for k in range(1, n):
            origin = lax.rem(z + k, n)
            total += jnp.dot(b_all[origin, c], metric_rows(origin), preferred_element_type=jnp.float32)
        table[q, c] = total.astype(table.dtype)
        share(c)

    def fit_far(c):
        first = jnp.where(low, 1, 0)
        tiles = depth // rows // 2
        total = None
        for j in range(2 * (n - 1)):
            lhs = b_all[first + j // 2, c, :, (j % 2) * tiles * rows:(j % 2 + 1) * tiles * rows]
            rhs = jnp.concatenate([far_metric[u // parts, u % parts] for u in range(j * tiles, (j + 1) * tiles)], axis=0)
            term = jnp.dot(lhs, rhs, preferred_element_type=jnp.float32)
            total = term if total is None else total + term
        fit_part[c] = total.astype(fit_part.dtype)
        half_fit(c).start()

    def fit_end(c):
        total = jnp.dot(b_all[z, c], metric_rows(z), preferred_element_type=jnp.float32)
        half_fit(c).wait_recv()
        table[q, c] = (total + fit_part[c].astype(jnp.float32)).astype(table.dtype)
        share(c)

    @pl.when(is_mid)
    def _():
        own(0).start()

    swap(0).start()
    load_rest.wait()
    for c in range(1, chunks):
        mask(c)

        @pl.when(is_mid)
        def _():
            if c < 2:
                own(c).start()
            if c < whole:
                swap(c).start()

    load_metric.wait()

    @pl.when(is_end)
    def _():
        for c in range(1, chunks):
            if c <= parts:
                metric_part(c - 1).start()
            swap(c).start()

        def stage(c, carry):
            @pl.when(c < whole)
            def _():
                swap(c, mate).wait_recv()
                for k in (0, 1):
                    raw_in(k, c).wait_recv()
                fit(c)

            @pl.when((c >= whole) & (c < chunks))
            def _():
                fit_end(c)

            @pl.when((c >= 2) & (c < chunks + 2))
            def _():
                pass_on(c - 2)

            @pl.when(c >= 4)
            def _():
                pass_corner(c - 4)
            return carry

        lax.fori_loop(0, chunks + 4, stage, 0)

    @pl.when(is_mid)
    def _():
        def stage(s, carry):
            @pl.when((s >= 1) & (s <= parts))
            def _():
                t = s - 1
                at = far_metric.at[q, t]
                remote(at, at, y_s.at[t], y_r.at[t], (z, partner)).wait_recv()
                m_share(t)

            @pl.when(s < chunks)
            def _():
                swap(s, mate).wait_recv()
                relay(s).start()

            @pl.when(s + 2 < chunks)
            def _():
                own(s + 2).start()

            @pl.when((s >= 2) & (s < parts + 2))
            def _():
                m_pass_on(s - 2)

            @pl.when((s >= 3) & (s < parts + 3))
            def _():
                m_pass_corner(s - 3)

            c = s - 2
            inside = (c >= 0) & (c < chunks)

            @pl.when(inside)
            def _():
                own(c, other).wait_recv()
                relay(c, n - 1 - mate).wait_recv()

            @pl.when(inside & (c < whole))
            def _():
                for k in (0, 1):
                    raw(k, c).start()

            @pl.when(inside & (c > whole))
            def _():
                fit_far(c)

            @pl.when(inside)
            def _():
                fit(c)

            @pl.when(c == whole)
            def _():
                for t in range(parts):
                    m_finish(t)
                fit_far(c)

            @pl.when((s >= 4) & (s < chunks + 4))
            def _():
                pass_on(s - 4)

            @pl.when(s >= 6)
            def _():
                pass_corner(s - 6)
            return carry

        lax.fori_loop(0, chunks + 6, stage, 0)

    def finish_all(c, carry):
        finish(c)
        return carry

    load_dom.wait()
    lax.fori_loop(0, chunks, finish_all, 0)

    row_of = lax.broadcasted_iota(jnp.int32, (width, width), 0)
    col_of = lax.broadcasted_iota(jnp.int32, (width, width), 1)

    half = width // 2

    def near(p):
        return remote(g_send.at[0, p], g_recv.at[0, p], g_s.at[0, p], g_r.at[0, p], (mate, q))

    def late(p):
        return remote(late_send.at[p], late_recv.at[p], g_s.at[0, p], g_r.at[0, p], (mate, q))

    lane = lax.broadcasted_iota(jnp.int32, (slab, half), 1)
    line = lax.broadcasted_iota(jnp.int32, (slab, half), 0)
    lower = (lane < slab) & (line >= lane)

    def pack(square):
        return jnp.where(lower, pltpu.roll(square[slab:], slab, 1), square[:slab])

    def to_mid(p):
        return remote(far_out.at[p], far_recv.at[p], x_s.at[p], x_r.at[p], (mate, q))

    def across(j, p):
        return remote(far_send.at[j, p], v_recv.at[p], c_s.at[j, p], g_r.at[1, p],
                      (jnp.where(z < 2, 2, 0) + j, q))

    def packed(p):
        return remote(far_send.at[2, p], t_recv.at[p], c_s.at[2, p], g_r.at[2, p], (other, q))

    def packed_on(p):
        return remote(t_recv.at[p], t_recv.at[p], g_s.at[1, p], g_r.at[2, p], (mate, q))

    def combine(below):
        def one(p, carry):
            to_mid(p).wait_recv()
            far_send[2, p] = (g_far[p, half:] + far_recv[p, half:].astype(jnp.float32)).astype(far_send.dtype)
            packed(p).start()
            value = (g_far[p, 0:half] + far_recv[p, 0:half].astype(jnp.float32).T).astype(far_send.dtype)
            for j in ((1, 0) if below else (0, 1)):
                far_send[j, p] = value[j * slab:(j + 1) * slab]
                across(j, p).start()

            @pl.when(p >= 2)
            def _():
                packed(p - 2).wait_recv()
                packed_on(p - 2).start()
            return carry
        lax.fori_loop(0, pairs, one, 0)
        for p in (pairs - 2, pairs - 1):
            packed(p).wait_recv()
            packed_on(p).start()

    def near_late(p, carry):
        late(p).start()
        return carry

    def gram(p, carry):
        blocks = []
        for s in range(slots):
            name = dom_ref[s, q * pairs + p]
            local = lax.rem(name, chunks // split) * split
            for t in range(split):
                blocks.append(table[name // (chunks // split), local + t])
        stack = jnp.concatenate(blocks, axis=0)
        full = lax.dot_general(stack, stack, (((1,), (1,)), ((), ())), preferred_element_type=jnp.float32)
        d_own[p] = jnp.sum(jnp.where(row_of == col_of, full, 0.0), axis=0, keepdims=True)
        for d in range(n):
            part = full[d * slab:(d + 1) * slab]

            @pl.when(z == d)
            def _():
                out_ref[p] = part

        for end, below in ((0, True), (3, False)):
            near_cols, far_cols = (slice(0, half), slice(half, width))[::1 if below else -1]
            mid = 1 if below else 2

            @pl.when(z == end)
            def _():
                far_out[p, 0:half] = full[near_cols, far_cols].astype(far_out.dtype)
                far_out[p, half:] = pack(full[far_cols, far_cols]).astype(far_out.dtype)
                late_send[p] = full[mid * slab:(mid + 1) * slab, near_cols].astype(late_send.dtype)
                to_mid(p).start()

            @pl.when(z == mid)
            def _():
                g_far[p, 0:half] = full[far_cols, near_cols]
                g_far[p, half:] = pack(full[far_cols, far_cols])
                g_send[0, p] = full[end * slab:(end + 1) * slab].astype(g_send.dtype)
                near(p).start()
        return carry

    lax.fori_loop(0, pairs, gram, 0)

    def diag_copy(k):
        return remote(d_own, d_recv.at[k - 1], d_s.at[k - 1], d_r.at[k - 1], (lax.rem(z + k, n), q))

    for k in range(1, n):
        diag_copy(k).start()
    @pl.when(is_end)
    def _():
        lax.fori_loop(0, pairs, near_late, 0)

    def drain_all(c, carry):
        drain(c)

        @pl.when(is_end | (c < whole))
        def _():
            swap(c).wait_send()

        @pl.when(is_mid)
        def _():
            own(c).wait_send()
            relay(c).wait_send()

            @pl.when(c < whole)
            def _():
                for k in (0, 1):
                    raw(k, c).wait_send()

            @pl.when(c >= whole)
            def _():
                half_fit(c).wait_send()
        return carry

    lax.fori_loop(0, chunks, drain_all, 0)
    for t in range(parts):
        @pl.when(is_end)
        def _():
            metric_part(t).wait_send()

        @pl.when(is_mid)
        def _():
            m_drain(t)

    for mid, below in ((1, True), (2, False)):
        @pl.when(z == mid)
        def _():
            combine(below)

    def leave(p):
        return pltpu.make_async_copy(out_ref.at[p], out_hbm.at[p], out_sem.at[p])

    leave_diag = pltpu.make_async_copy(diag_ref, diag_hbm, in_sem.at[3])
    for k in range(1, n):
        diag_copy(k).wait_recv()

    diag = d_own[...]
    for k in range(1, n):
        diag += d_recv[k - 1]
    diag_ref[...] = diag
    leave_diag.start()

    def add(p, carry):
        across(0, p).wait_recv()

        @pl.when(is_end)
        def _():
            packed(p).wait_recv()

        tied = t_recv[p].astype(jnp.float32)
        twice = jnp.concatenate((tied, tied), axis=0).T
        cross = v_recv[p].astype(jnp.float32)
        for d in range(n):
            @pl.when(z == d)
            def _():
                if d % 2 == 0:
                    side = jnp.where(lower, twice[:slab], tied)
                else:
                    side = jnp.where(line < lane - slab, twice[:slab], pltpu.roll(tied, slab, 1))
                    side = jnp.where(lane < slab, twice[slab:], side)
                total = out_ref[p] + jnp.concatenate((side, cross) if d < 2 else (cross, side), axis=1)
                if d in (0, n - 1):
                    near(p).wait_recv()
                    out_ref[p] = total + g_recv[0, p].astype(jnp.float32)
                else:
                    late(p).wait_recv()
                    pieces = (late_recv[p], far_recv[p, d % 2 * slab:(d % 2 + 1) * slab])
                    whole_row = jnp.concatenate(pieces if d < 2 else pieces[::-1], axis=1)
                    out_ref[p] = total + whole_row.astype(jnp.float32)

        leave(p).start()
        return carry

    lax.fori_loop(0, pairs, add, 0)

    def drain_gram(p, carry):
        leave(p).wait()

        @pl.when(is_end)
        def _():
            late(p).wait_send()
            to_mid(p).wait_send()

        @pl.when(is_mid)
        def _():
            near(p).wait_send()
            for j in range(2):
                across(j, p).wait_send()
            packed(p).wait_send()
            packed_on(p).wait_send()
        return carry

    lax.fori_loop(0, pairs, drain_gram, 0)
    leave_diag.wait()
    for k in range(1, n):
        diag_copy(k).wait_send()


def close_kernel(rows, total_ref, diag_ref, cnt_ref, out_ref):
    pairs, slab, width = out_ref.shape
    slab_row = lax.broadcasted_iota(jnp.int32, (slab, width), 0) + lax.axis_index("aux") * slab
    slab_col = lax.broadcasted_iota(jnp.int32, (slab, width), 1)
    last = jnp.maximum(slab_row, slab_col)

    def close(p, carry):
        value = jnp.where(slab_row == slab_col, diag_ref[p], total_ref[p])
        out_ref[p] = jnp.where(last < cnt_ref[p] * rows, value, 0.0)
        return carry

    lax.fori_loop(0, pairs, close, 0)


def per_device(n, n_pair, b_three, metric, aux_map, domains, counts):
    rows_dev, aux_dev = b_three.shape
    blocks_dev, aux_blocks = aux_map.shape
    width_cw = rows_dev // blocks_dev
    pairs = counts.shape[0]
    slots = domains.shape[1]
    width = slots * width_cw
    slab = width // n
    split = 1
    chunks = blocks_dev * split
    chunk_rows = width_cw // split
    columns = metric.shape[1]
    chips = n_pair // 2
    box = n == 4 and n_pair == 8
    parts = (n - 1) * aux_dev // (n_pair * chunk_rows)
    vmem = pl.BlockSpec(memory_space=pltpu.VMEM)
    smem = pl.BlockSpec(memory_space=pltpu.SMEM)
    dma = pltpu.SemaphoreType.DMA
    hbm = pl.BlockSpec(memory_space=pl.ANY)
    bf16 = jnp.bfloat16
    scratch = [pltpu.VMEM((chunks, chunk_rows, aux_dev), bf16) for _ in range(1 if box else 2)] + [
        pltpu.VMEM(metric.shape, bf16),
        dma((5,)),
        pltpu.VMEM((n, chunks, chunk_rows, aux_dev), bf16),
        pltpu.VMEM((n_pair, chunks, chunk_rows, columns), bf16),
    ]
    grams = [
        pltpu.VMEM((1 if box else n, pairs, slab, width), bf16),
        pltpu.VMEM((1 if box else n - 1, pairs, slab, width), bf16),
        pltpu.VMEM((pairs, 1, width), jnp.float32),
        pltpu.VMEM((n - 1, pairs, 1, width), jnp.float32),
    ]
    gram_sems = [dma((n - 1, pairs)), dma((n - 1, pairs)), dma((n - 1,)), dma((n - 1,))]
    specs, outs = [hbm, hbm, vmem, smem], (vmem, vmem)
    if box:
        body = box_kernel
        specs, outs = [hbm] * 4, (hbm, hbm)
        scratch = [
            pltpu.VMEM(aux_map.shape, jnp.int32),
            pltpu.SMEM((slots, domains.shape[0]), jnp.int32),
            pltpu.VMEM((pairs, slab, width), jnp.float32),
            pltpu.VMEM((pairs, 1, width), jnp.float32),
            dma((pairs,)),
        ] + scratch
        scratch += [
            pltpu.VMEM((n_pair, parts, chunk_rows, columns), bf16),
            pltpu.VMEM((chunks, chunk_rows, columns), bf16),
            dma((chunks,)), dma((chunks,)), dma((2, chunks)), dma((2, chunks)), dma((2, chunks)), dma((2, chunks)),
            dma((chunks,)), dma((chunks,)), dma((parts,)), dma((parts,)),
        ]
        for count in (chunks, parts):
            scratch += [dma((k, count)) for k in (3, 3, 2, 2, 3, 3)]
        scratch += grams + gram_sems + [
            pltpu.VMEM((pairs, width - slab, width // 2), jnp.float32),
            pltpu.VMEM((pairs, width - slab, width // 2), bf16),
            pltpu.VMEM((pairs, width - slab, width // 2), bf16),
            pltpu.VMEM((3, pairs, slab, width // 2), bf16),
            pltpu.VMEM((pairs, slab, width // 2), bf16),
            pltpu.VMEM((pairs, slab, width // 2), bf16),
            pltpu.VMEM((pairs, slab, width // 2), bf16),
            pltpu.VMEM((pairs, slab, width // 2), bf16),
            dma((pairs,)), dma((pairs,)), dma((3, pairs)),
        ]
    else:
        body = line_kernel
        scratch += grams + [dma((n - 1, chunks)) for _ in range(4)] + [dma((chips, chunks)) for _ in range(4)] + gram_sems
    total, diag = pl.pallas_call(
        functools.partial(body, n, n_pair, split),
        out_shape=(jax.ShapeDtypeStruct((pairs, slab, width), jnp.float32),
                   jax.ShapeDtypeStruct((pairs, 1, width), jnp.float32)),
        in_specs=specs,
        out_specs=outs,
        scratch_shapes=scratch,
        compiler_params=pltpu.CompilerParams(
            collective_id=0, has_side_effects=True, vmem_limit_bytes=60 * 1024 * 1024),
    )(b_three.reshape(chunks, chunk_rows, aux_dev), metric, aux_map, domains.T)
    return pl.pallas_call(
        functools.partial(close_kernel, width_cw),
        out_shape=jax.ShapeDtypeStruct((pairs, slab, width), jnp.float32),
        in_specs=[vmem, vmem, smem],
        out_specs=vmem,
    )(total, diag, counts)


def solution(mesh):
    return jax.shard_map(
        functools.partial(per_device, mesh.shape["aux"], mesh.shape["pair"]),
        mesh=mesh,
        in_specs=(P("pair", "aux"), P(None, "aux"), P("pair", "aux"), P(), P("pair")),
        out_specs=P("pair", "aux", None),
        check_vma=False,
    )
```
